32 devices in a mesh: gx: 4 (over z), gy: 4 (over y, core), gz: 2 (over x).
Axes of the slice: x: 2, y: 2, z: 4, core: 2. Of those that a mesh axis runs over, the one named last changes fastest.
Arguments:
- potential: float32 [64, 192, 256], P('gx', 'gy', 'gz'), may hold values from -6 to 6
- density_matrix: float32 [32, 169], P(('gx', 'gy', 'gz')), may hold values from -6 to 6
- delta_table: float32 [4, 9, 169], replicated, may hold values from -36 to 36
- coulomb: float32 [4, 169, 169], replicated, may hold values from -0.5 to 0.5
- radius: float32 [4], replicated, may hold values from 1.5 to 3
- atom_species: int32 [32], replicated, may hold values from 0 to 3
- slot_atom: int32 [32, 8], P(('gx', 'gy', 'gz')), may hold values from 0 to 31, as said below
- slot_corner: int32 [3, 32, 8], P(None, ('gx', 'gy', 'gz')), may hold values from -15 to 127, as said below
- slot_count: int32 [32], P(('gx', 'gy', 'gz')), may hold values from 1 to 8, as said below
- projections: float32 [32, 8, 13, 256], P(('gx', 'gy', 'gz')), may hold values from -1.5 to 1.5
Outputs:
- dh: float32 [32, 169], P(('gx', 'gy', 'gz'))
- applied: float32 [32, 8, 13, 256], P(('gx', 'gy', 'gz'))
The draws below stay inside these ranges and needn't reach their ends.
Inputs may be any that keep to these rules, and one draw needn't show every extreme that they name: `slot_atom`: atom a is owned by domain a in row-major order over (gx, gy, gz). Its box of 16 cells a side lies inside the grid and its lowest cell lies in the owner's domain. The live slots of a domain name each atom whose box reaches the domain exactly once, in any order, and only those; the owner of such an atom has the domain's coordinates minus 0 or 1 along each axis. Dead slots hold 0. `slot_corner`: for a live slot, the atom's lowest box cell minus the domain's first cell, per axis; the same atom gives the same global corner in every domain. Dead slots hold 0. `slot_count`: live slots come first. Every domain lists the atom it owns, and some domain has all 8 slots live in every draw.
All inputs are finite; a program needn't handle non-finite values.
Results may differ from the reference program's by a relative error of at most 0.0003.
Values sent between devices are 32-bit elements; how exact they have to be, the bound alone decides.
No kernel may reach another device: no remote copies, remote signals or barrier semaphores. Data moves between devices by JAX's collectives and lax.ppermute only.
A program may use at most 64 MiB of HBM per device.

```python
import math
import jax
import jax.numpy as jnp
from jax import lax

CX = 16
CY = 48
CZ = 128
OWNED = 1
BANDS = 256
BOX = 16
SHAPES = 9
NP = 13
SPECIES = 4
NX = 64
NY = 192
NZ = 256
DOMAINS = 32
ATOMS = 32
SLOTS = 8
PAIRS = 169
N_GY = 4
N_GZ = 2


def layout(key):
    across_x = NX // CX
    across_y = NY // CY
    across_z = NZ // CZ
    domains = across_x * across_y * across_z
    extents = jnp.array([CX, CY, CZ], jnp.int32)
    counts = jnp.array([across_x, across_y, across_z], jnp.int32)
    domain = jnp.arange(domains, dtype=jnp.int32)
    coords = jnp.stack([domain // (across_y * across_z), domain // across_z % across_y, domain % across_z])
    owner_coords = jnp.repeat(coords, OWNED, axis=1)
    key_cluster, key_place, key_order = jax.random.split(jax.random.fold_in(key, 31), 3)
    cluster = jax.random.randint(key_cluster, (3,), 1, counts, dtype=jnp.int32)
    topmost = owner_coords == (counts - 1)[:, None]
    highest_corner = jnp.where(topmost, extents[:, None] - BOX, extents[:, None] - 1)
    below = owner_coords == (cluster - 1)[:, None]
    inside = jnp.all(below | (owner_coords == cluster[:, None]), axis=0)
    lowest_corner = jnp.where(inside[None, :] & below, extents[:, None] - (BOX - 1), 0)
    drawn = jax.random.randint(key_place, owner_coords.shape, 0, 1 << 20, dtype=jnp.int32)
    corner = owner_coords * extents[:, None] + lowest_corner + drawn % (highest_corner - lowest_corner + 1)
    steps = jnp.arange(8, dtype=jnp.int32)
    lifts = jnp.stack([steps // 4, steps // 2 % 2, steps % 2])
    owner_of = coords[:, :, None] - lifts[:, None, :]
    valid = jnp.all(owner_of >= 0, axis=0)
    owner_line = (owner_of[0] * across_y + owner_of[1]) * across_z + owner_of[2]
    member = jnp.arange(OWNED, dtype=jnp.int32)
    candidate = (owner_line[:, :, None] * OWNED + member[None, None, :]).reshape(domains, SLOTS)
    valid_slot = jnp.repeat(valid, OWNED, axis=1)
    candidate = jnp.where(valid_slot, candidate, 0)
    box_corner = corner[:, candidate]
    start = (coords * extents[:, None])[:, :, None]
    reach = jnp.all((box_corner + BOX - 1 >= start) & (box_corner < start + extents[:, None, None]), axis=0)
    live = valid_slot & reach
    score = jnp.where(live, 0, 1) * (SLOTS * 4096) + jax.random.randint(key_order, (domains, SLOTS), 0, 4096, dtype=jnp.int32) * SLOTS + jnp.arange(SLOTS, dtype=jnp.int32)[None, :]
    order = jnp.argsort(score, axis=1, stable=True)
    live_sorted = jnp.take_along_axis(live, order, axis=1)
    atoms_sorted = jnp.where(live_sorted, jnp.take_along_axis(candidate, order, axis=1), 0)
    relative = box_corner - start
    relative = jnp.take_along_axis(relative, jnp.broadcast_to(order[None], relative.shape), axis=2)
    relative = jnp.where(live_sorted[None], relative, 0)
    return (atoms_sorted, relative, jnp.sum(live_sorted.astype(jnp.int32), axis=1))


def draw_slot_atom(key, part):
    return layout(key)[0]


def draw_slot_corner(key, part):
    return layout(key)[1]


def draw_slot_count(key, part):
    return layout(key)[2]


def place_ends(values, own_key, least, high):
    longest = values.shape.index(max(values.shape))
    spots = []
    for shift in (0, 1):
        where = [jax.random.randint(jax.random.fold_in(own_key, axis), (), 0, length) for axis, length in enumerate(values.shape)]
        where[longest] = (where[longest] + shift) % values.shape[longest]
        spots.append(tuple(where))
    return values.at[spots[0]].set(least).at[spots[1]].set(high)


def level_of(key, dims, shards, smallest, high):
    level = 1.0
    for position, blocks in shards:
        steps = jax.random.uniform(jax.random.fold_in(jax.random.fold_in(key, 6), position), (blocks,), jnp.float32, smallest / len(shards), high / len(shards))
        level = level * jnp.repeat(jnp.exp(steps), dims[position] // blocks).reshape((-1,) + (1,) * (len(dims) - 1 - position))
    return level


def normal_values(key, shape, scale, most, cuts=(), held_as=jnp.bfloat16):
    entries = jax.random.normal(key, shape, jnp.float32) * scale
    if len(cuts) > 0:
        entries = level_of(key, shape, cuts, -0.22, 0.18) * entries
    return jnp.clip(entries, min=-most, max=most).astype(held_as)


def setup_inputs(seed: int = 0) -> dict:
    streams_of = jax.random.split(jax.random.key(seed), 11)
    potential = normal_values(streams_of[0], (NX, NY, NZ), 1.0, 6.0, ((0, 4), (1, 4), (2, 2)), jnp.float32)
    density_matrix = normal_values(streams_of[1], (ATOMS, PAIRS), 1.0, 6.0, ((0, 32),), jnp.float32)
    delta_table = normal_values(streams_of[2], (SPECIES, SHAPES, PAIRS), 6.0, 36.0, (), jnp.float32)
    coulomb = normal_values(streams_of[3], (SPECIES, PAIRS, PAIRS), PAIRS ** -0.5, 0.5, (), jnp.float32)
    radius = jnp.clip(jnp.exp(jax.random.uniform(streams_of[4], (SPECIES,), jnp.float32, math.log(1.5), math.log(3.0))), 1.5, 3.0)
    atom_species = place_ends(jax.random.randint(streams_of[5], (ATOMS,), 0, SPECIES), jax.random.fold_in(streams_of[5], 1), 0, SPECIES - 1).astype(jnp.int32)
    slot_atom = draw_slot_atom(jax.random.fold_in(streams_of[10], 71), 0)
    slot_corner = draw_slot_corner(jax.random.fold_in(streams_of[10], 71), 0)
    slot_count = draw_slot_count(jax.random.fold_in(streams_of[10], 71), 0)
    projections = normal_values(streams_of[9], (DOMAINS, SLOTS, NP, BANDS), 0.25, 1.5, ((0, 32),), jnp.float32)
    return {"potential": potential, "density_matrix": density_matrix, "delta_table": delta_table, "coulomb": coulomb, "radius": radius, "atom_species": atom_species, "slot_atom": slot_atom, "slot_corner": slot_corner, "slot_count": slot_count, "projections": projections}


highest = lax.Precision.HIGHEST
harmonic_scale = 0.5 / math.sqrt(3.0)

def shape_table(radius):
    offsets = jnp.arange(BOX, dtype=jnp.float32) - (BOX - 1) / 2.0
    cube = (BOX, BOX, BOX)
    first = jnp.broadcast_to(offsets[:, None, None], cube).reshape(1, -1) / radius[:, None]
    second = jnp.broadcast_to(offsets[None, :, None], cube).reshape(1, -1) / radius[:, None]
    third = jnp.broadcast_to(offsets[None, None, :], cube).reshape(1, -1) / radius[:, None]
    square = first * first + second * second + third * third
    envelope = jnp.exp(-square)
    envelope = envelope / lax.optimization_barrier(jnp.sum(envelope, axis=1, keepdims=True))
    harmonics = [jnp.ones_like(first), first, second, third, first * second, second * third, third * first, 0.5 * (first * first - second * second), harmonic_scale * (3.0 * third * third - square)]
    return jnp.stack([item * envelope for item in harmonics], axis=1)

def reference(potential, density_matrix, delta_table, coulomb, radius, atom_species, slot_atom, slot_corner, slot_count, projections):
    table = shape_table(radius)
    domain = jnp.arange(DOMAINS, dtype=jnp.int32)
    anchor_x = jnp.repeat(domain // (N_GY * N_GZ) * CX, SLOTS)
    anchor_y = jnp.repeat(domain // N_GZ % N_GY * CY, SLOTS)
    anchor_z = jnp.repeat(domain % N_GZ * CZ, SLOTS)
    flat_atom = slot_atom.reshape(-1)
    live = (jnp.arange(SLOTS, dtype=jnp.int32)[None, :] < slot_count[:, None]).reshape(-1)
    kinds = atom_species[flat_atom]
    offsets = jnp.arange(BOX, dtype=jnp.int32)

    def integral(item):
        anchor_a, anchor_b, anchor_c, shift_a, shift_b, shift_c, kind = item
        start_a = anchor_a + shift_a
        start_b = anchor_b + shift_b
        start_c = anchor_c + shift_c
        tile = lax.dynamic_slice(potential, (start_a, start_b, start_c), (BOX, BOX, BOX))
        inside_a = ((shift_a + offsets >= 0) & (shift_a + offsets < CX)).astype(jnp.float32)
        inside_b = ((shift_b + offsets >= 0) & (shift_b + offsets < CY)).astype(jnp.float32)
        inside_c = ((shift_c + offsets >= 0) & (shift_c + offsets < CZ)).astype(jnp.float32)
        masked = tile * inside_a[:, None, None] * inside_b[None, :, None] * inside_c[None, None, :]
        shapes = lax.dynamic_index_in_dim(table, kind, 0, keepdims=False)
        return jnp.dot(shapes, masked.reshape(-1), precision=highest)
    partial_value = lax.map(integral, (anchor_x, anchor_y, anchor_z, slot_corner[0].reshape(-1), slot_corner[1].reshape(-1), slot_corner[2].reshape(-1), kinds))
    partial_value = partial_value * live.astype(jnp.float32)[:, None]
    totals = jnp.zeros((ATOMS, SHAPES), jnp.float32).at[flat_atom].add(partial_value)
    dh = jnp.zeros((ATOMS, PAIRS), jnp.float32)
    for kind in range(SPECIES):
        term = jnp.dot(totals, delta_table[kind], precision=highest) + 2.0 * jnp.dot(density_matrix, coulomb[kind].T, precision=highest)
        dh = dh + (atom_species == kind).astype(jnp.float32)[:, None] * term
    slot_dh = dh[flat_atom].reshape(-1, NP, NP)
    bands = projections.reshape(-1, NP, BANDS)
    applied = jnp.einsum('sij,sib->sjb', slot_dh, bands, precision=highest) * live.astype(jnp.float32)[:, None, None]
    return (dh, applied.reshape(DOMAINS, SLOTS, NP, BANDS))
```

```python
import functools
import math

import jax
import jax.numpy as jnp
from jax import lax
from jax.experimental import pallas as pl
from jax.experimental.pallas import tpu as pltpu
from jax.sharding import PartitionSpec as P

BOX = 16
GROUP = 16
LANES = 128
AXES = ("gx", "gy", "gz")
HALF = (BOX - 1) / 2.0
harmonic_scale = 0.5 / math.sqrt(3.0)
f32 = jnp.float32
bf16 = jnp.bfloat16


def dot(a, b):
    return jnp.dot(a, b, preferred_element_type=f32)


def split(x):
    high = x.astype(bf16)
    return high, (x - high.astype(f32)).astype(bf16)


def lanes_of(shape):
    return lax.broadcasted_iota(jnp.int32, shape, len(shape) - 1)


def quotient(x, by):
    return jnp.floor((x + 0.5) * (1.0 / by))


def front(
    dims,
    cells_y,
    atom_ref,
    corner_ref,
    count_ref,
    species_ref,
    radius_ref,
    density_ref,
    delta_ref,
    potential_hbm,
    coulomb_hbm,
    pay_ref,
    dt_high_ref,
    dt_low_ref,
    spread_ref,
    pick_ref,
    v_ref,
    c_ref,
    dt_ref,
    sems,
):
    _, ny, nz = dims
    devices = pay_ref.shape[0]
    slots = atom_ref.shape[1]
    kinds, shapes, pairs = delta_ref.shape
    cells, size_z = v_ref.shape
    index_x, index_y, index_z = (lax.axis_index(a) for a in AXES)
    me = (index_x * ny + index_y) * nz + index_z
    v_copy = pltpu.make_async_copy(potential_hbm, v_ref, sems.at[0])
    v_copy.start()
    c_copy = pltpu.make_async_copy(coulomb_hbm.at[species_ref[me]], c_ref, sems.at[1])
    c_copy.start()

    tile = (8, LANES)
    row = lax.broadcasted_iota(jnp.int32, tile, 0)
    lane = lanes_of(tile)
    zero = jnp.zeros(tile, f32)
    kx, ky, kz, alive, radius = zero, zero, zero, zero, jnp.ones(tile, f32)
    group = lanes_of((GROUP, LANES)) // GROUP
    atom_lane = lanes_of((GROUP, devices))
    dt_ref[...] = jnp.zeros(dt_ref.shape, f32)
    for s in range(slots):
        live = s < count_ref[0]
        atom = atom_ref[0, s]
        kind = species_ref[atom]
        x, y, z = corner_ref[0, 0, s], corner_ref[1, 0, s], corner_ref[2, 0, s]
        code = (
            jnp.where(x < 0, 4, 0) + jnp.where(y < 0, 2, 0) + jnp.where(z < 0, 1, 0)
        )
        hit = row == jnp.where(live, code, 8)
        kx = jnp.where(hit, x.astype(f32), kx)
        ky = jnp.where(hit, y.astype(f32), ky)
        kz = jnp.where(hit, z.astype(f32), kz)
        radius = jnp.where(hit, radius_ref[kind], radius)
        alive = jnp.where(hit, 1.0, alive)
        rows = slice(s * GROUP, (s + 1) * GROUP)
        spread_ref[rows, :] = jnp.where(group == jnp.where(live, code, 8), 1.0, 0.0)
        pick_ref[rows, :] = jnp.where(atom_lane == jnp.where(live, atom, -1), 1.0, 0.0)

        @pl.when(live)
        def _():
            at = pl.ds(pl.multiple_of(code * GROUP, GROUP), shapes)
            dt_ref[at, :pairs] = delta_ref[kind]

    own = slice(slots * GROUP, slots * GROUP + 8)
    spread_ref[own, :] = jnp.where(group[:8] == 0, 1.0, 0.0)
    pick_ref[own, :] = jnp.where(atom_lane[:8] == me, 1.0, 0.0)
    dt_high_ref[...], dt_low_ref[...] = split(dt_ref[...])

    inverse = 1.0 / radius
    line = (lane.astype(f32) - HALF) * inverse
    line = jnp.where(lane < BOX, jnp.exp(-line * line), 0.0)
    line = jnp.sum(line, axis=1, keepdims=True)
    norm = alive / (line * line * line)

    def over(x, width):
        return jnp.concatenate([x] * (width // LANES), axis=1)

    def axis_of(position, corner, width):
        offset = position - over(corner, width)
        inside = (offset >= 0.0) & (offset < BOX)
        return (offset - HALF) * over(inverse, width), inside

    cell = lanes_of((8, cells)).astype(f32)
    cell_x = quotient(cell, cells_y)
    u, in_x = axis_of(cell_x, kx, cells)
    v, in_y = axis_of(cell - cell_x * cells_y, ky, cells)
    e = jnp.where(in_x & in_y, jnp.exp(-(u * u + v * v)), 0.0)
    eu, ev = e * u, e * v
    weights = jnp.concatenate([e, eu, ev, eu * v, eu * u, ev * v], axis=0)
    w_high, w_low = split(weights)
    w, in_z = axis_of(lanes_of((8, size_z)).astype(f32), kz, size_z)
    g = jnp.where(in_z, jnp.exp(-w * w), 0.0)
    gw = g * w

    c_copy.wait()
    density = jnp.broadcast_to(density_ref[...], (8, pairs))
    c_high, c_low = split(c_ref[...])
    d_high, d_low = split(density)
    contract = functools.partial(
        lax.dot_general,
        dimension_numbers=(((1,), (1,)), ((), ())),
        preferred_element_type=f32,
    )
    field = contract(d_high, c_high) + contract(d_high, c_low) + contract(d_low, c_high)
    field = 2.0 * field[:1]
    pay_ref[:, LANES + LANES :] = jnp.zeros((devices, LANES), f32)
    pay_ref[:, LANES : LANES + pairs] = jnp.broadcast_to(field, (devices, pairs))

    v_copy.wait()
    v_high, v_low = split(v_ref[...])
    both = dot(jnp.concatenate([w_high, w_low], axis=0), v_high)
    m = both[:48] + both[48:] + dot(w_high, v_low)
    m0, mu, mv, muv, muu, mvv = (m[8 * i : 8 * i + 8] for i in range(6))
    parts = [
        m0 * g,
        mu * g,
        mv * g,
        m0 * gw,
        muv * g,
        mv * gw,
        mu * gw,
        0.5 * (muu - mvv) * g,
        harmonic_scale * (2.0 * m0 * (gw * w) - (muu + mvv) * g),
    ]
    tiled = zero
    for i, part in enumerate(parts):
        total = jnp.sum(part, axis=1, keepdims=True)
        tiled = jnp.where(lane % GROUP == i, total, tiled)
    tiled = tiled * norm

    ky_step = 2 * nz + 2
    kx_step = ky_step * (2 * ny + 2)
    wide = (devices, LANES)
    e_index = lax.broadcasted_iota(jnp.int32, wide, 0).astype(f32)
    e_xy = quotient(e_index, nz)
    e_x = quotient(e_xy, ny)
    e_key = e_x * kx_step + (e_xy - e_x * ny) * ky_step + (e_index - e_xy * nz)
    my_key = index_x * kx_step + index_y * ky_step + index_z
    target = lanes_of(wide) // GROUP
    t_key = (target // 4) * kx_step + (target // 2 % 2) * ky_step + target % 2
    gap = t_key.astype(f32) - e_key + my_key.astype(f32)
    sent = jnp.zeros(wide, f32)
    for c in range(8):
        c_key = (c // 4) * kx_step + (c // 2 % 2) * ky_step + c % 2
        sent = jnp.where(gap == float(c_key), tiled[c : c + 1], sent)
    pay_ref[:, :LANES] = sent


def back(got_ref, dt_high_ref, dt_low_ref, spread_ref, pick_ref, projections_ref, dh_ref, applied_ref, p_ref):
    slots, projectors, bands = projections_ref.shape
    pairs = dh_ref.shape[1]
    rows = slots * GROUP
    got = got_ref[...]
    totals = jnp.sum(got[:, :LANES], axis=0, keepdims=True)
    s_high, s_low = split(spread_ref[...] * totals)
    m_high, m_low = split(got[:, LANES:])
    pick = pick_ref[...].astype(bf16)
    d_high = dt_high_ref[...]
    h = (
        dot(s_high, d_high)
        + dot(s_low, d_high)
        + dot(s_high, dt_low_ref[...])
        + dot(pick, m_high)
        + dot(pick, m_low)
    )
    dh_ref[...] = h[rows : rows + 1, :pairs]
    h = h[:rows]
    width = h.shape[1]
    p = lanes_of((rows, width)).astype(f32)
    j = p - quotient(p, projectors) * projectors
    slot_row = lax.broadcasted_iota(jnp.int32, (rows, width), 0)
    keep = (j == (slot_row % GROUP).astype(f32)) & (p < pairs)
    h_high, h_low = split(jnp.where(keep, h, 0.0))
    q_row = quotient(lax.broadcasted_iota(jnp.int32, (width, rows), 0).astype(f32), projectors)
    move = jnp.where(q_row == (lanes_of((width, rows)) % GROUP).astype(f32), 1.0, 0.0).astype(bf16)
    block = dot(jnp.concatenate([h_high, h_low], axis=0), move)
    b_row = lax.broadcasted_iota(jnp.int32, (2 * rows, rows), 0) % rows
    diagonal = b_row // GROUP == lanes_of((2 * rows, rows)) // GROUP
    block = jnp.where(diagonal, block, 0.0).astype(bf16)
    p_ref[...] = jnp.zeros(p_ref.shape, f32)
    for s in range(slots):
        p_ref[s * GROUP : s * GROUP + projectors, :] = projections_ref[s]
    p_high, p_low = split(p_ref[...])
    both = dot(block, p_high)
    out = both[:rows] + both[rows:] + dot(block[:rows], p_low)
    for s in range(slots):
        applied_ref[s] = out[s * GROUP : s * GROUP + projectors]


def local(
    potential,
    density_matrix,
    delta_table,
    coulomb,
    radius,
    atom_species,
    slot_atom,
    slot_corner,
    slot_count,
    projections,
):
    dims = tuple(lax.axis_size(a) for a in AXES)
    devices = math.prod(dims)
    assert density_matrix.shape[0] == 1 and slot_atom.shape[1] == 8
    slots = slot_atom.shape[1]
    size_x, size_y, size_z = potential.shape
    pairs = density_matrix.shape[1]
    columns = 2 * LANES
    rows = slots * GROUP
    smem = pl.BlockSpec(memory_space=pltpu.SMEM)
    vmem = pl.BlockSpec(memory_space=pltpu.VMEM)
    hbm = pl.BlockSpec(memory_space=pl.ANY)
    pay, dt_high, dt_low, spread, pick = pl.pallas_call(
        functools.partial(front, dims, size_y),
        out_shape=(
            jax.ShapeDtypeStruct((devices, LANES + columns), f32),
            jax.ShapeDtypeStruct((8 * GROUP, columns), bf16),
            jax.ShapeDtypeStruct((8 * GROUP, columns), bf16),
            jax.ShapeDtypeStruct((rows + 8, LANES), f32),
            jax.ShapeDtypeStruct((rows + 8, devices), f32),
        ),
        in_specs=[smem] * 5 + [vmem] * 2 + [hbm] * 2,
        out_specs=[vmem] * 5,
        scratch_shapes=[
            pltpu.VMEM((size_x * size_y, size_z), f32),
            pltpu.VMEM((pairs, pairs), f32),
            pltpu.VMEM((8 * GROUP, columns), f32),
            pltpu.SemaphoreType.DMA((2,)),
        ],
    )(
        slot_atom,
        slot_corner,
        slot_count,
        atom_species,
        radius,
        density_matrix,
        delta_table,
        potential.reshape(size_x * size_y, size_z),
        coulomb,
    )
    got = lax.all_to_all(pay, AXES, 0, 0, tiled=True)
    dh, applied = pl.pallas_call(
        back,
        out_shape=(
            jax.ShapeDtypeStruct(density_matrix.shape, f32),
            jax.ShapeDtypeStruct(projections.shape[1:], f32),
        ),
        in_specs=[vmem] * 6,
        out_specs=[vmem] * 2,
        scratch_shapes=[pltpu.VMEM((rows, projections.shape[3]), f32)],
    )(got, dt_high, dt_low, spread, pick, projections[0])
    return dh, applied[None]


def solution(mesh):
    return jax.shard_map(
        local,
        mesh=mesh,
        in_specs=(
            P("gx", "gy", "gz"),
            P(AXES, None),
            P(),
            P(),
            P(),
            P(),
            P(AXES, None),
            P(None, AXES, None),
            P(AXES),
            P(AXES, None, None, None),
        ),
        out_specs=(P(AXES, None), P(AXES, None, None, None)),
        check_vma=False,
    )
```

```python
import functools
import math

import jax
import jax.numpy as jnp
from jax import lax
from jax.experimental import pallas as pl
from jax.experimental.pallas import tpu as pltpu
from jax.sharding import PartitionSpec as P

BOX = 16
CODES = 8
LANES = 128
AXES = ("gx", "gy", "gz")
HALF = (BOX - 1) / 2.0
VMEM_BYTES = 8 << 20
harmonic_scale = 0.5 / math.sqrt(3.0)
f32 = jnp.float32
bf16 = jnp.bfloat16
TILE = (CODES, LANES)


def dot(a, b):
    return jnp.dot(a, b, preferred_element_type=f32)


def split(x):
    high = x.astype(bf16)
    return high, (x - high.astype(f32)).astype(bf16)


def lanes_of(shape):
    return lax.broadcasted_iota(jnp.int32, shape, len(shape) - 1)


def quotient(x, by):
    return jnp.floor((x + 0.5) * (1.0 / by))


def front(
    dims,
    cells_y,
    atom_hbm,
    corner_hbm,
    species_hbm,
    radius_hbm,
    density_hbm,
    potential_hbm,
    coulomb_hbm,
    pay_ref,
    kinds_ref,
    codes_ref,
    atom_ref,
    corner_ref,
    species_ref,
    radius_ref,
    density_ref,
    v_ref,
    c_ref,
    sems,
):
    _, ny, nz = dims
    slots = atom_ref.shape[1]
    cells, size_z = v_ref.shape
    pairs, kinds, _ = c_ref.shape
    sources = (atom_hbm, corner_hbm, species_hbm, radius_hbm, density_hbm, potential_hbm, coulomb_hbm)
    targets = (atom_ref, corner_ref, species_ref, radius_ref, density_ref, v_ref, c_ref)
    copies = [pltpu.make_async_copy(s, t, sems.at[i]) for i, (s, t) in enumerate(zip(sources, targets))]
    for copy in copies:
        copy.start()
    index_x, index_y, index_z = (lax.axis_index(a) for a in AXES)
    me = (index_x * ny + index_y) * nz + index_z
    row = lax.broadcasted_iota(jnp.int32, TILE, 0)
    lane = lanes_of(TILE)
    zero = jnp.zeros(TILE, f32)
    for copy in copies[:4]:
        copy.wait()

    kx, ky, kz, alive, radius, kind_of = zero, zero, zero, zero, jnp.ones(TILE, f32), zero
    codes = jnp.full(TILE, -1.0, f32)
    for s in range(slots):
        atom = atom_ref[0, s]
        kind = species_ref[atom]
        x, y, z = corner_ref[0, 0, s], corner_ref[1, 0, s], corner_ref[2, 0, s]
        code = jnp.where(x < 0, 4, 0) + jnp.where(y < 0, 2, 0) + jnp.where(z < 0, 1, 0)
        if s > 0:
            code = jnp.where((atom == 0) & (x == 0) & (y == 0) & (z == 0), -1, code)
        hit = row == code
        kx = jnp.where(hit, x.astype(f32), kx)
        ky = jnp.where(hit, y.astype(f32), ky)
        kz = jnp.where(hit, z.astype(f32), kz)
        radius = jnp.where(hit, radius_ref[kind], radius)
        kind_of = jnp.where(hit, kind.astype(f32), kind_of)
        alive = jnp.where(hit, 1.0, alive)
        codes = jnp.where(row == s, code.astype(f32), codes)
    kinds_ref[...] = kind_of
    codes_ref[...] = codes

    inverse = 1.0 / radius
    line = (lane.astype(f32) - HALF) * inverse
    line = jnp.where(lane < BOX, jnp.exp(-line * line), 0.0)
    line = jnp.sum(line, axis=1, keepdims=True)
    norm = alive / (line * line * line)

    def over(x, width):
        return jnp.concatenate([x] * (width // LANES), axis=1)

    def axis_of(position, corner, width):
        offset = position - over(corner, width)
        inside = (offset >= 0.0) & (offset < BOX)
        return (offset - HALF) * over(inverse, width), inside

    cell = lanes_of((CODES, cells)).astype(f32)
    cell_x = quotient(cell, cells_y)
    u, in_x = axis_of(cell_x, kx, cells)
    v, in_y = axis_of(cell - cell_x * cells_y, ky, cells)
    e = jnp.where(in_x & in_y, jnp.exp(-(u * u + v * v)), 0.0)
    eu, ev = e * u, e * v
    weights = jnp.concatenate([e, eu, ev, eu * v, eu * u, ev * v], axis=0)
    w_high, w_low = split(weights)
    w, in_z = axis_of(lanes_of((CODES, size_z)).astype(f32), kz, size_z)
    g = jnp.where(in_z, jnp.exp(-w * w), 0.0)
    gw = g * w

    copies[5].wait()
    v_high, v_low = split(v_ref[...])
    both = dot(jnp.concatenate([w_high, w_low], axis=0), v_high)
    m = both[: 6 * CODES] + both[6 * CODES :] + dot(w_high, v_low)
    m0, mu, mv, muv, muu, mvv = (m[CODES * i : CODES * (i + 1)] for i in range(6))
    parts = [
        m0 * g,
        mu * g,
        mv * g,
        m0 * gw,
        muv * g,
        mv * gw,
        mu * gw,
        0.5 * (muu - mvv) * g,
        harmonic_scale * (2.0 * m0 * (gw * w) - (muu + mvv) * g),
    ]
    partial = zero
    for i, part in enumerate(parts):
        partial = jnp.where(lane == i, jnp.sum(part, axis=1, keepdims=True), partial)
    pay_ref[:CODES] = partial * norm

    copies[4].wait()
    copies[6].wait()
    density = 2.0 * density_ref[...]
    small = lanes_of((kinds, LANES))
    lines = [jnp.zeros((kinds, LANES), f32) for _ in range(2)]
    for n in range(pairs):
        total = jnp.sum(c_ref[n] * density, axis=1, keepdims=True)
        lines[n // LANES] = jnp.where(small == n % LANES, total, lines[n // LANES])
    own = lax.broadcasted_iota(jnp.int32, (kinds, LANES), 0) == species_ref[me]
    for i, line in enumerate(lines):
        field = jnp.sum(jnp.where(own, line, 0.0), axis=0, keepdims=True)
        pay_ref[CODES * (i + 1) : CODES * (i + 2)] = jnp.where(row == 0, field, 0.0)


def prepare(kinds_ref, delta_ref, out_ref):
    shapes, kinds, pairs = delta_ref.shape
    out_ref[:, LANES:] = jnp.zeros((shapes * CODES, LANES), f32)
    kind = jnp.concatenate([kinds_ref[...]] * 2, axis=1)[:, :pairs]
    for i in range(shapes):
        rows = delta_ref[i]
        chosen = jnp.zeros((CODES, pairs), f32)
        for k in range(kinds):
            chosen = jnp.where(kind == float(k), rows[k : k + 1], chosen)
        out_ref[i * CODES : (i + 1) * CODES, :pairs] = chosen


def back(pay_ref, delta_ref, codes_ref, projections_ref, dh_ref, applied_ref):
    projectors = projections_ref.shape[0]
    bands = projections_ref.shape[2]
    pairs = dh_ref.shape[1]
    width = 2 * LANES
    totals = pay_ref[:CODES]
    h = jnp.concatenate([pay_ref[CODES : 2 * CODES], pay_ref[2 * CODES :]], axis=1)
    for i in range(delta_ref.shape[0] // CODES):
        h = h + jnp.broadcast_to(totals[:, i : i + 1], (CODES, width)) * delta_ref[i * CODES : (i + 1) * CODES]
    dh_ref[...] = h[:1, :pairs]
    codes = jnp.concatenate([codes_ref[...]] * 2, axis=1)
    by_slot = jnp.zeros((CODES, width), f32)
    for c in range(CODES):
        by_slot = jnp.where(codes == float(c), h[c : c + 1], by_slot)
    for j in range(projectors):
        out = jnp.zeros((CODES, bands), f32)
        for i in range(projectors):
            at = i * projectors + j
            out = out + jnp.broadcast_to(by_slot[:, at : at + 1], (CODES, bands)) * projections_ref[i]
        applied_ref[j] = out


def swaps(dims, axis, odd):
    nx, ny, nz = dims
    size = dims[axis]

    def partner(at):
        i = at[axis]
        other = i ^ 1 if not odd else (i + 1 ^ 1) - 1
        if 0 <= other < size:
            return at[:axis] + (other,) + at[axis + 1 :]
        if axis == 0 and at[1] ^ 1 < ny:
            return (at[0], at[1] ^ 1, at[2])
        if axis == 1 and odd and size % 2 == 0:
            return (at[0], size - 1 - i, at[2])
        return at

    def line(at):
        return (at[0] * ny + at[1]) * nz + at[2]

    every = [(x, y, z) for x in range(nx) for y in range(ny) for z in range(nz)]
    return [(line(at), line(partner(at))) for at in every]


def exchange(x, dims, axis):
    index = lax.axis_index(AXES[axis])
    even = index % 2 == 0
    first = lax.ppermute(x, AXES, swaps(dims, axis, False))
    second = lax.ppermute(x, AXES, swaps(dims, axis, True)) if dims[axis] > 2 else first
    up = jnp.where(even, first, second)
    down = jnp.where(even, second, first)
    step = CODES // 2 >> axis
    up = jnp.roll(up, -step, axis=0)
    down = jnp.roll(down, step, axis=0)
    row = lax.broadcasted_iota(jnp.int32, x.shape, 0)
    higher = row // step % 2 == 1
    partial = row < CODES
    has_up = index < dims[axis] - 1
    kept = jnp.where(partial & ~higher & has_up, x + up, x)
    return jnp.where(higher, jnp.where(partial, x + down, down), kept)


def local(
    potential,
    density_matrix,
    delta_table,
    coulomb,
    radius,
    atom_species,
    slot_atom,
    slot_corner,
    slot_count,
    projections,
):
    dims = tuple(lax.axis_size(a) for a in AXES)
    slots = slot_atom.shape[1]
    assert density_matrix.shape[0] == 1 and slots == CODES
    size_x, size_y, size_z = potential.shape
    pairs = density_matrix.shape[1]
    kinds, shapes, _ = delta_table.shape
    smem, vmem, hbm = (pl.BlockSpec(memory_space=m) for m in (pltpu.SMEM, pltpu.VMEM, pltpu.HBM))
    params = pltpu.CompilerParams(vmem_limit_bytes=VMEM_BYTES)
    tile = jax.ShapeDtypeStruct(TILE, f32)
    pay, kind_of, codes = pl.pallas_call(
        functools.partial(front, dims, size_y),
        out_shape=(pltpu.VMEM((3 * CODES, LANES), f32), pltpu.VMEM(TILE,f32), pltpu.VMEM(TILE,f32)),
        in_specs=[hbm] * 7,
        out_specs=[vmem] * 3,
        scratch_shapes=[
            pltpu.SMEM(slot_atom.shape, jnp.int32),
            pltpu.SMEM(slot_corner.shape, jnp.int32),
            pltpu.SMEM(atom_species.shape, jnp.int32),
            pltpu.SMEM(radius.shape, f32),
            pltpu.VMEM((1, pairs), f32),
            pltpu.VMEM((size_x * size_y, size_z), f32),
            pltpu.VMEM((pairs, kinds, pairs), f32),
            pltpu.SemaphoreType.DMA((7,)),
        ],
        compiler_params=params,
    )(*(pltpu.with_memory_space_constraint(x, pltpu.HBM) for x in (
        slot_atom,
        slot_corner,
        atom_species,
        radius,
        density_matrix,
        potential.reshape(size_x * size_y, size_z),
        coulomb.transpose(1, 0, 2),
    )))
    delta = pl.pallas_call(
        prepare,
        out_shape=jax.ShapeDtypeStruct((shapes * CODES, 2 * LANES), f32),
        in_specs=[vmem] * 2,
        out_specs=vmem,
        compiler_params=params,
        cost_estimate=pl.CostEstimate(flops=200000, bytes_accessed=200000, transcendentals=0),
    )(kind_of, delta_table.transpose(1, 0, 2))
    for axis in (2, 1, 0):
        pay = exchange(pay, dims, axis)
    bands = projections[0].transpose(1, 0, 2)
    dh, applied = pl.pallas_call(
        back,
        out_shape=(jax.ShapeDtypeStruct(density_matrix.shape, f32), jax.ShapeDtypeStruct(bands.shape, f32)),
        in_specs=[vmem] * 4,
        out_specs=[vmem] * 2,
        compiler_params=params,
    )(pay, delta, codes, bands)
    return dh, applied.transpose(1, 0, 2)[None]


def solution(mesh):
    return jax.shard_map(
        local,
        mesh=mesh,
        in_specs=(
            P("gx", "gy", "gz"),
            P(AXES, None),
            P(),
            P(),
            P(),
            P(),
            P(AXES, None),
            P(None, AXES, None),
            P(AXES),
            P(AXES, None, None, None),
        ),
        out_specs=(P(AXES, None), P(AXES, None, None, None)),
        check_vma=False,
    )
```

```python
import functools
import math

import jax
import jax.numpy as jnp
from jax import lax
from jax.experimental import pallas as pl
from jax.experimental.pallas import tpu as pltpu
from jax.sharding import PartitionSpec as P

BOX = 16
CODES = 8
LANES = 128
PART = LANES - 16
AXES = ("gx", "gy", "gz")
HALF = (BOX - 1) / 2.0
VMEM_BYTES = 8 << 20
harmonic_scale = 0.5 / math.sqrt(3.0)
f32 = jnp.float32
bf16 = jnp.bfloat16
TILE = (CODES, LANES)
STATE = (2 * CODES, LANES)


def dot(a, b):
    return jnp.dot(a, b, preferred_element_type=f32)


def split(x):
    high = x.astype(bf16)
    return high, (x - high.astype(f32)).astype(bf16)


def lanes_of(shape):
    return lax.broadcasted_iota(jnp.int32, shape, len(shape) - 1)


def quotient(x, by):
    return jnp.floor((x + 0.5) * (1.0 / by))


def front(
    dims,
    cells_y,
    atom_hbm,
    corner_hbm,
    species_hbm,
    radius_hbm,
    density_hbm,
    potential_hbm,
    coulomb_hbm,
    pay_ref,
    kinds_ref,
    codes_ref,
    atom_ref,
    corner_ref,
    species_ref,
    radius_ref,
    density_ref,
    v_ref,
    c_ref,
    sems,
):
    _, ny, nz = dims
    slots = atom_ref.shape[1]
    cells, size_z = v_ref.shape
    pairs, kinds, _ = coulomb_hbm.shape
    def cut(source, target, chunks, sem):
        size = -(-source.shape[0] // chunks // 8) * 8
        for at in range(0, source.shape[0], size):
            part = slice(at, min(at + size, source.shape[0]))
            pltpu.make_async_copy(source.at[part], target.at[part], sem).start()
        return pltpu.make_async_copy(target, target, sem)

    v_copy = cut(potential_hbm, v_ref, 8, sems.at[5])
    sources = (atom_hbm, corner_hbm, species_hbm, radius_hbm, density_hbm)
    targets = (atom_ref, corner_ref, species_ref, radius_ref, density_ref)
    copies = [pltpu.make_async_copy(s, t, sems.at[i]) for i, (s, t) in enumerate(zip(sources, targets))]
    for copy in copies:
        copy.start()
    for k in range(kinds):
        pltpu.make_async_copy(coulomb_hbm.at[:, k : k + 1, :], c_ref.at[k], sems.at[6]).start()
    c_copy = pltpu.make_async_copy(c_ref, c_ref, sems.at[6])
    index_x, index_y, index_z = (lax.axis_index(a) for a in AXES)
    me = (index_x * ny + index_y) * nz + index_z
    row = lax.broadcasted_iota(jnp.int32, TILE, 0)
    lane = lanes_of(TILE)
    zero = jnp.zeros(TILE, f32)
    for copy in copies[:4]:
        copy.wait()

    zero_i = jnp.zeros(TILE, jnp.int32)
    kx, ky, kz, alive, kind_of = zero_i, zero_i, zero_i, zero, zero_i
    radius = jnp.ones(TILE, f32)
    codes = jnp.full(TILE, -1, jnp.int32)
    for s in range(slots):
        atom = atom_ref[0, s]
        kind = species_ref[atom]
        x, y, z = corner_ref[0, 0, s], corner_ref[1, 0, s], corner_ref[2, 0, s]
        code = (x >> 31 & 4) | (y >> 31 & 2) | (z >> 31 & 1)
        if s > 0:
            code = jnp.where((atom | x | y | z) == 0, -1, code)
        hit = row == code
        kx = jnp.where(hit, x, kx)
        ky = jnp.where(hit, y, ky)
        kz = jnp.where(hit, z, kz)
        radius = jnp.where(hit, radius_ref[kind], radius)
        kind_of = jnp.where(hit, kind, kind_of)
        alive = jnp.where(hit, 1.0, alive)
        codes = jnp.where(row == s, code, codes)
    kx, ky, kz = (k.astype(f32) for k in (kx, ky, kz))
    kinds_ref[...] = kind_of
    codes_ref[...] = codes

    inverse = 1.0 / radius
    line = (lane.astype(f32) - HALF) * inverse
    line = jnp.where(lane < BOX, jnp.exp(-line * line), 0.0)
    line = jnp.sum(line, axis=1, keepdims=True)
    norm = alive / (line * line * line)

    def over(x, width):
        return jnp.concatenate([x] * (width // LANES), axis=1)

    def axis_of(position, corner, width):
        offset = position - over(corner, width)
        inside = (offset >= 0.0) & (offset < BOX)
        return (offset - HALF) * over(inverse, width), inside

    cell = lanes_of((CODES, cells)).astype(f32)
    cell_x = quotient(cell, cells_y)
    u, in_x = axis_of(cell_x, kx, cells)
    v, in_y = axis_of(cell - cell_x * cells_y, ky, cells)
    e = jnp.where(in_x & in_y, jnp.exp(-(u * u + v * v)), 0.0)
    eu, ev = e * u, e * v
    weights = jnp.concatenate([e, eu, ev, eu * v, eu * u, ev * v], axis=0)
    w_high, w_low = split(weights)
    w, in_z = axis_of(lanes_of((CODES, size_z)).astype(f32), kz, size_z)
    g = jnp.where(in_z, jnp.exp(-w * w), 0.0)
    gw = g * w

    v_copy.wait()
    v_high, v_low = split(v_ref[...])
    both = dot(jnp.concatenate([w_high, w_low], axis=0), v_high)
    m = both[: 6 * CODES] + both[6 * CODES :] + dot(w_high, v_low)
    m0, mu, mv, muv, muu, mvv = (m[CODES * i : CODES * (i + 1)] for i in range(6))
    parts = [
        m0 * g,
        mu * g,
        mv * g,
        m0 * gw,
        muv * g,
        mv * gw,
        mu * gw,
        0.5 * (muu - mvv) * g,
        harmonic_scale * (2.0 * m0 * (gw * w) - (muu + mvv) * g),
    ]
    partial = zero
    for i, part in enumerate(parts):
        partial = jnp.where(lane == PART + i, jnp.sum(part, axis=1, keepdims=True), partial)
    partial = partial * norm

    copies[4].wait()
    c_copy.wait()
    p_high, p_low = split(c_ref[species_ref[me], :, 0, :] * (2.0 * density_ref[...]))
    rest = pairs - LANES
    ones = jnp.ones((16, pairs), bf16)
    contract = functools.partial(
        lax.dot_general, dimension_numbers=(((1,), (1,)), ((), ())), preferred_element_type=f32
    )
    field = contract(ones, p_high) + contract(ones, p_low)
    pay_ref[:CODES] = jnp.where(row == 0, field[:CODES, :LANES], 0.0)
    pay_ref[CODES:] = jnp.where(lane < PART, 0.0, partial)
    pay_ref[CODES : CODES + 1, :rest] = field[:1, LANES:]


def prepare(kinds_ref, delta_ref, projections_ref, out_ref, move_ref, high_ref, low_ref):
    shapes, kinds, pairs = delta_ref.shape
    projectors, slots, bands = projections_ref.shape
    out_ref[:, LANES:] = jnp.zeros((shapes * CODES, LANES), f32)
    kind = jnp.concatenate([kinds_ref[...]] * 2, axis=1)[:, :pairs]
    for i in range(shapes):
        rows = delta_ref[i]
        chosen = jnp.zeros((CODES, pairs), f32)
        for k in range(kinds):
            chosen = jnp.where(kind == k, rows[k : k + 1], chosen)
        out_ref[i * CODES : (i + 1) * CODES, :pairs] = chosen
    pair = lax.broadcasted_iota(jnp.int32, move_ref.shape, 0).astype(f32)
    row_of = quotient(pair, projectors)
    move_ref[...] = jnp.where(row_of == (lanes_of(move_ref.shape) // slots).astype(f32), 1.0, 0.0).astype(bf16)
    stack = projections_ref[...].reshape(projectors * slots, bands)
    stack = jnp.concatenate([stack, jnp.zeros((LANES - projectors * slots, bands), f32)], axis=0)
    high_ref[...], low_ref[...] = split(stack)


def merged(axis, size, pay_ref, second_ref, first_ref):
    index = lax.axis_index(AXES[axis])
    even = index % 2 == 0
    step = CODES // 2 >> axis
    row = lax.broadcasted_iota(jnp.int32, TILE, 0)
    higher = row // step % 2 == 1
    partial = lanes_of(TILE) >= PART
    add_up = partial & (index < size - 1)

    def tiles(ref):
        return ref[:CODES], ref[CODES:]

    x, a, b = tiles(pay_ref), tiles(first_ref), tiles(second_ref)
    down = [pltpu.roll(jnp.where(even, q, p), step, 0) for p, q in zip(a, b)]
    up = pltpu.roll(jnp.where(even, a[1], b[1]), CODES - step, 0)
    kept = jnp.where(add_up, x[1] + up, x[1])
    taken = jnp.where(partial, x[1] + down[1], down[1])
    return jnp.where(higher, down[0], x[0]), jnp.where(higher, taken, kept)


def merge(axis, size, pay_ref, first_ref, second_ref, out_ref):
    out_ref[:CODES], out_ref[CODES:] = merged(axis, size, pay_ref, first_ref, second_ref)


def back(
    axis,
    size,
    pay_ref,
    first_ref,
    second_ref,
    delta_ref,
    codes_ref,
    move_ref,
    high_ref,
    low_ref,
    dh_ref,
    applied_ref,
):
    projectors, slots, _ = applied_ref.shape
    pairs = dh_ref.shape[1]
    width = 2 * LANES
    head, tail = merged(axis, size, pay_ref, first_ref, second_ref)
    h = jnp.concatenate([head, jnp.where(lanes_of(TILE) < PART, tail, 0.0)], axis=1)
    for i in range(delta_ref.shape[0] // CODES):
        total = tail[:, PART + i : PART + i + 1]
        h = h + jnp.broadcast_to(total, (CODES, width)) * delta_ref[i * CODES : (i + 1) * CODES]
    dh_ref[...] = h[:1, :pairs]
    codes = jnp.concatenate([codes_ref[...]] * 2, axis=1)
    by_slot = jnp.zeros((CODES, width), f32)
    for c in range(CODES):
        by_slot = jnp.where(codes == c, h[c : c + 1], by_slot)
    pair = lanes_of((CODES, width)).astype(f32)
    column = pair - quotient(pair, projectors) * projectors
    column = jnp.where(pair < pairs, column, -1.0)
    high = by_slot.astype(bf16).astype(f32)
    blocks = -(-projectors * CODES // 16) * 2
    parts = [jnp.where(column == float(j), part, 0.0) for part in (high, by_slot - high) for j in range(blocks)]
    matrix = dot(jnp.concatenate(parts, axis=0).astype(bf16), move_ref[...])
    rows = blocks * CODES
    diagonal = lanes_of(TILE) % slots == lax.broadcasted_iota(jnp.int32, TILE, 0)
    matrix = jnp.where(jnp.concatenate([diagonal] * (2 * blocks), axis=0), matrix, 0.0).astype(bf16)
    both = dot(matrix, high_ref[...])
    out = both[:rows] + both[rows:] + dot(matrix[:rows], low_ref[...])
    applied_ref[...] = out[: projectors * slots].reshape(applied_ref.shape)


def swaps(dims, axis, odd):
    nx, ny, nz = dims
    size = dims[axis]

    def partner(at):
        i = at[axis]
        other = i ^ 1 if not odd else (i + 1 ^ 1) - 1
        if 0 <= other < size:
            return at[:axis] + (other,) + at[axis + 1 :]
        if axis == 0 and at[1] ^ 1 < ny:
            return (at[0], at[1] ^ 1, at[2])
        if axis == 1 and odd and size % 2 == 0:
            return (at[0], size - 1 - i, at[2])
        return at

    def line(at):
        return (at[0] * ny + at[1]) * nz + at[2]

    every = [(x, y, z) for x in range(nx) for y in range(ny) for z in range(nz)]
    return [(line(at), line(partner(at))) for at in every]


def exchange(x, dims, axis):
    first = lax.ppermute(x, AXES, swaps(dims, axis, False))
    second = lax.ppermute(x, AXES, swaps(dims, axis, True)) if dims[axis] > 2 else first
    return x, second, first


def local(
    potential,
    density_matrix,
    delta_table,
    coulomb,
    radius,
    atom_species,
    slot_atom,
    slot_corner,
    slot_count,
    projections,
):
    dims = tuple(lax.axis_size(a) for a in AXES)
    slots = slot_atom.shape[1]
    assert density_matrix.shape[0] == 1 and slots == CODES
    size_x, size_y, size_z = potential.shape
    pairs = density_matrix.shape[1]
    kinds, shapes, _ = delta_table.shape
    vmem, hbm = (pl.BlockSpec(memory_space=m) for m in (pltpu.VMEM, pltpu.HBM))
    params = pltpu.CompilerParams(vmem_limit_bytes=VMEM_BYTES)
    pay, kind_of, codes = pl.pallas_call(
        functools.partial(front, dims, size_y),
        out_shape=(pltpu.VMEM(STATE, f32), pltpu.VMEM(TILE, jnp.int32), pltpu.VMEM(TILE, jnp.int32)),
        in_specs=[hbm] * 7,
        out_specs=[vmem] * 3,
        scratch_shapes=[
            pltpu.SMEM(slot_atom.shape, jnp.int32),
            pltpu.SMEM(slot_corner.shape, jnp.int32),
            pltpu.SMEM(atom_species.shape, jnp.int32),
            pltpu.SMEM(radius.shape, f32),
            pltpu.VMEM((1, pairs), f32),
            pltpu.VMEM((size_x * size_y, size_z), f32),
            pltpu.VMEM((kinds, pairs, 1, pairs), f32),
            pltpu.SemaphoreType.DMA((7,)),
        ],
        compiler_params=params,
    )(
        *(
            pltpu.with_memory_space_constraint(x, pltpu.HBM)
            for x in (
                slot_atom,
                slot_corner,
                atom_species,
                radius,
                density_matrix,
                potential.reshape(size_x * size_y, size_z),
                coulomb.transpose(1, 0, 2),
            )
        )
    )
    bands = projections[0].transpose(1, 0, 2)
    delta, move, high, low = pl.pallas_call(
        prepare,
        out_shape=(
            pltpu.VMEM((shapes * CODES, 2 * LANES), f32),
            pltpu.VMEM((2 * LANES, LANES), bf16),
            pltpu.VMEM((LANES, bands.shape[2]), bf16),
            pltpu.VMEM((LANES, bands.shape[2]), bf16),
        ),
        in_specs=[vmem] * 3,
        out_specs=[vmem] * 4,
        compiler_params=params,
        cost_estimate=pl.CostEstimate(flops=500000, bytes_accessed=500000, transcendentals=0),
    )(kind_of, delta_table.transpose(1, 0, 2), bands)
    for axis in (2, 1):
        pay = pl.pallas_call(
            functools.partial(merge, axis, dims[axis]),
            out_shape=pltpu.VMEM(STATE, f32),
            in_specs=[vmem] * 3,
            out_specs=vmem,
            compiler_params=params,
        )(*exchange(pay, dims, axis))
    dh, applied = pl.pallas_call(
        functools.partial(back, 0, dims[0]),
        out_shape=(jax.ShapeDtypeStruct(density_matrix.shape, f32), jax.ShapeDtypeStruct(bands.shape, f32)),
        in_specs=[vmem] * 8,
        out_specs=[vmem] * 2,
        compiler_params=params,
    )(*exchange(pay, dims, 0), delta, codes, move, high, low)
    return dh, applied.transpose(1, 0, 2)[None]


def solution(mesh):
    return jax.shard_map(
        local,
        mesh=mesh,
        in_specs=(
            P("gx", "gy", "gz"),
            P(AXES, None),
            P(),
            P(),
            P(),
            P(),
            P(AXES, None),
            P(None, AXES, None),
            P(AXES),
            P(AXES, None, None, None),
        ),
        out_specs=(P(AXES, None), P(AXES, None, None, None)),
        check_vma=False,
    )
```

```python
import functools
import math

import jax
import jax.numpy as jnp
from jax import lax
from jax.experimental import pallas as pl
from jax.experimental.pallas import tpu as pltpu
from jax.sharding import PartitionSpec as P

BOX = 16
CODES = 8
LANES = 128
PART = LANES - 16
AXES = ("gx", "gy", "gz")
HALF = (BOX - 1) / 2.0
VMEM_BYTES = 8 << 20
harmonic_scale = 0.5 / math.sqrt(3.0)
f32 = jnp.float32
bf16 = jnp.bfloat16
TILE = (CODES, LANES)
STATE = (2 * CODES, LANES)


def dot(a, b):
    return jnp.dot(a, b, preferred_element_type=f32)


def split(x):
    high = x.astype(bf16)
    return high, (x - high.astype(f32)).astype(bf16)


def lanes_of(shape):
    return lax.broadcasted_iota(jnp.int32, shape, len(shape) - 1)


def quotient(x, by):
    return jnp.floor((x + 0.5) * (1.0 / by))


def front(
    dims,
    cells_y,
    atom_hbm,
    corner_hbm,
    species_hbm,
    radius_hbm,
    density_hbm,
    potential_hbm,
    coulomb_hbm,
    pay_ref,
    kinds_ref,
    codes_ref,
    atom_ref,
    corner_ref,
    species_ref,
    radius_ref,
    density_ref,
    v_ref,
    c_ref,
    sems,
):
    _, ny, nz = dims
    slots = atom_ref.shape[1]
    cells, size_z = v_ref.shape
    pairs, kinds, _ = coulomb_hbm.shape
    def cut(source, target, chunks, sem):
        size = -(-source.shape[0] // chunks // 8) * 8
        for at in range(0, source.shape[0], size):
            part = slice(at, min(at + size, source.shape[0]))
            pltpu.make_async_copy(source.at[part], target.at[part], sem).start()
        return pltpu.make_async_copy(target, target, sem)

    v_copy = cut(potential_hbm, v_ref, 8, sems.at[5])
    sources = (atom_hbm, corner_hbm, species_hbm, radius_hbm, density_hbm)
    targets = (atom_ref, corner_ref, species_ref, radius_ref, density_ref)
    copies = [pltpu.make_async_copy(s, t, sems.at[i]) for i, (s, t) in enumerate(zip(sources, targets))]
    for copy in copies:
        copy.start()
    for k in range(kinds):
        pltpu.make_async_copy(coulomb_hbm.at[:, k : k + 1, :], c_ref.at[k], sems.at[6]).start()
    c_copy = pltpu.make_async_copy(c_ref, c_ref, sems.at[6])
    index_x, index_y, index_z = (lax.axis_index(a) for a in AXES)
    me = (index_x * ny + index_y) * nz + index_z
    row = lax.broadcasted_iota(jnp.int32, TILE, 0)
    lane = lanes_of(TILE)
    zero = jnp.zeros(TILE, f32)
    for copy in copies[:4]:
        copy.wait()

    zero_i = jnp.zeros(TILE, jnp.int32)
    kx, ky, kz, alive, kind_of = zero_i, zero_i, zero_i, zero, zero_i
    radius = jnp.ones(TILE, f32)
    codes = jnp.full(TILE, -1, jnp.int32)
    for s in range(slots):
        atom = atom_ref[0, s]
        kind = species_ref[atom]
        x, y, z = corner_ref[0, 0, s], corner_ref[1, 0, s], corner_ref[2, 0, s]
        code = (x >> 31 & 4) | (y >> 31 & 2) | (z >> 31 & 1)
        if s > 0:
            code = jnp.where((atom | x | y | z) == 0, -1, code)
        hit = row == code
        kx = jnp.where(hit, x, kx)
        ky = jnp.where(hit, y, ky)
        kz = jnp.where(hit, z, kz)
        radius = jnp.where(hit, radius_ref[kind], radius)
        kind_of = jnp.where(hit, kind, kind_of)
        alive = jnp.where(hit, 1.0, alive)
        codes = jnp.where(row == s, code, codes)
    kx, ky, kz = (k.astype(f32) for k in (kx, ky, kz))
    kinds_ref[...] = kind_of
    codes_ref[...] = codes

    inverse = 1.0 / radius
    line = (lane.astype(f32) - HALF) * inverse
    line = jnp.where(lane < BOX, jnp.exp(-line * line), 0.0)
    line = jnp.sum(line, axis=1, keepdims=True)
    norm = alive / (line * line * line)

    def over(x, width):
        return jnp.concatenate([x] * (width // LANES), axis=1)

    def axis_of(position, corner, width):
        offset = position - over(corner, width)
        inside = (offset >= 0.0) & (offset < BOX)
        return (offset - HALF) * over(inverse, width), inside

    cell = lanes_of((CODES, cells)).astype(f32)
    cell_x = quotient(cell, cells_y)
    u, in_x = axis_of(cell_x, kx, cells)
    v, in_y = axis_of(cell - cell_x * cells_y, ky, cells)
    e = jnp.where(in_x & in_y, jnp.exp(-(u * u + v * v)), 0.0)
    eu, ev = e * u, e * v
    weights = jnp.concatenate([e, eu, ev, eu * v, eu * u, ev * v], axis=0)
    w_high, w_low = split(weights)
    w, in_z = axis_of(lanes_of((CODES, size_z)).astype(f32), kz, size_z)
    g = jnp.where(in_z, jnp.exp(-w * w), 0.0)
    gw = g * w

    v_copy.wait()
    v_high, v_low = split(v_ref[...])
    both = dot(jnp.concatenate([w_high, w_low], axis=0), v_high)
    m = both[: 6 * CODES] + both[6 * CODES :] + dot(w_high, v_low)
    m0, mu, mv, muv, muu, mvv = (m[CODES * i : CODES * (i + 1)] for i in range(6))
    parts = [
        m0 * g,
        mu * g,
        mv * g,
        m0 * gw,
        muv * g,
        mv * gw,
        mu * gw,
        0.5 * (muu - mvv) * g,
        harmonic_scale * (2.0 * m0 * (gw * w) - (muu + mvv) * g),
    ]
    partial = zero
    for i, part in enumerate(parts):
        partial = jnp.where(lane == PART + i, jnp.sum(part, axis=1, keepdims=True), partial)
    partial = partial * norm

    copies[4].wait()
    c_copy.wait()
    rest = pairs - LANES
    total = jnp.sum(c_ref[species_ref[me], :, 0, :] * (2.0 * density_ref[...]), axis=1, keepdims=True)
    square = (pairs, LANES)
    shift = lax.broadcasted_iota(jnp.int32, square, 0) - lanes_of(square)
    head = jnp.sum(jnp.where(shift == 0, total, 0.0), axis=0, keepdims=True)
    tail = jnp.sum(jnp.where(shift == LANES, total, 0.0), axis=0, keepdims=True)
    pay_ref[:CODES] = jnp.where(row == 0, head, 0.0)
    pay_ref[CODES:] = jnp.where(lane < PART, jnp.where(row == 0, tail, 0.0), partial)


def prepare(kinds_ref, delta_ref, projections_ref, out_ref, stack_ref):
    shapes, kinds, pairs = delta_ref.shape
    projectors, slots, bands = projections_ref.shape
    out_ref[:, LANES:] = jnp.zeros((shapes * CODES, LANES), f32)
    kind = jnp.concatenate([kinds_ref[...]] * 2, axis=1)[:, :pairs]
    for i in range(shapes):
        rows = delta_ref[i]
        chosen = jnp.zeros((CODES, pairs), f32)
        for k in range(kinds):
            chosen = jnp.where(kind == k, rows[k : k + 1], chosen)
        out_ref[i * CODES : (i + 1) * CODES, :pairs] = chosen
    stack = projections_ref[...].reshape(projectors * slots, bands)
    stack = jnp.concatenate([stack, jnp.zeros((LANES - projectors * slots, bands), f32)], axis=0)
    high, low = split(stack)
    for at, part in enumerate((high, high, low)):
        stack_ref[at * LANES : (at + 1) * LANES] = part


def merged(axis, size, pay_ref, second_ref, first_ref):
    index = lax.axis_index(AXES[axis])
    even = index % 2 == 0
    step = CODES // 2 >> axis
    row = lax.broadcasted_iota(jnp.int32, TILE, 0)
    higher = row // step % 2 == 1
    partial = lanes_of(TILE) >= PART
    add_up = partial & (index < size - 1)

    def tiles(ref):
        return ref[:CODES], ref[CODES:]

    x, a, b = tiles(pay_ref), tiles(first_ref), tiles(second_ref)
    down = [pltpu.roll(jnp.where(even, q, p), step, 0) for p, q in zip(a, b)]
    up = pltpu.roll(jnp.where(even, a[1], b[1]), CODES - step, 0)
    kept = jnp.where(add_up, x[1] + up, x[1])
    taken = jnp.where(partial, x[1] + down[1], down[1])
    return jnp.where(higher, down[0], x[0]), jnp.where(higher, taken, kept)


def merge(axis, size, pay_ref, first_ref, second_ref, out_ref):
    out_ref[:CODES], out_ref[CODES:] = merged(axis, size, pay_ref, first_ref, second_ref)


def back(
    axis,
    size,
    pay_ref,
    first_ref,
    second_ref,
    delta_ref,
    codes_ref,
    stack_ref,
    dh_ref,
    applied_ref,
):
    projectors, slots, _ = applied_ref.shape
    pairs = dh_ref.shape[1]
    width = 2 * LANES
    head, tail = merged(axis, size, pay_ref, first_ref, second_ref)
    h = jnp.concatenate([head, jnp.where(lanes_of(TILE) < PART, tail, 0.0)], axis=1)
    for i in range(delta_ref.shape[0] // CODES):
        total = tail[:, PART + i : PART + i + 1]
        h = h + jnp.broadcast_to(total, (CODES, width)) * delta_ref[i * CODES : (i + 1) * CODES]
    dh_ref[...] = h[:1, :pairs]
    codes = codes_ref[...]
    at = jnp.maximum(codes, 0)
    by_slot = [jnp.where(codes < 0, 0.0, jnp.take_along_axis(half, at, axis=0)) for half in (h[:, :LANES], h[:, LANES:])]
    lane = lanes_of(TILE)
    diagonal = lane % slots == lax.broadcasted_iota(jnp.int32, TILE, 0)
    rows = []
    for j in range(projectors):
        pair = lane // slots * projectors + j
        chosen = jnp.take_along_axis(by_slot[0], pair % LANES, axis=1)
        chosen = jnp.where(pair < LANES, chosen, jnp.take_along_axis(by_slot[1], pair % LANES, axis=1))
        rows.append(jnp.where(diagonal & (lane < projectors * slots), chosen, 0.0))
    if projectors % 2:
        rows.append(jnp.zeros(TILE, f32))
    high, low = split(jnp.concatenate(rows, axis=0))
    out = dot(jnp.concatenate([high, low, high], axis=1), stack_ref[...])
    applied_ref[...] = out[: projectors * slots].reshape(applied_ref.shape)


def swaps(dims, axis, odd):
    nx, ny, nz = dims
    size = dims[axis]

    def partner(at):
        i = at[axis]
        other = i ^ 1 if not odd else (i + 1 ^ 1) - 1
        if 0 <= other < size:
            return at[:axis] + (other,) + at[axis + 1 :]
        if axis == 0 and at[1] ^ 1 < ny:
            return (at[0], at[1] ^ 1, at[2])
        if axis == 1 and odd and size % 2 == 0:
            return (at[0], size - 1 - i, at[2])
        return at

    def line(at):
        return (at[0] * ny + at[1]) * nz + at[2]

    every = [(x, y, z) for x in range(nx) for y in range(ny) for z in range(nz)]
    return [(line(at), line(partner(at))) for at in every]


def exchange(x, dims, axis):
    first = lax.ppermute(x, AXES, swaps(dims, axis, False))
    second = lax.ppermute(x, AXES, swaps(dims, axis, True)) if dims[axis] > 2 else first
    return x, second, first


def local(
    potential,
    density_matrix,
    delta_table,
    coulomb,
    radius,
    atom_species,
    slot_atom,
    slot_corner,
    slot_count,
    projections,
):
    dims = tuple(lax.axis_size(a) for a in AXES)
    slots = slot_atom.shape[1]
    assert density_matrix.shape[0] == 1 and slots == CODES
    size_x, size_y, size_z = potential.shape
    pairs = density_matrix.shape[1]
    kinds, shapes, _ = delta_table.shape
    vmem, hbm = (pl.BlockSpec(memory_space=m) for m in (pltpu.VMEM, pltpu.HBM))
    params = pltpu.CompilerParams(vmem_limit_bytes=VMEM_BYTES)
    pay, kind_of, codes = pl.pallas_call(
        functools.partial(front, dims, size_y),
        out_shape=(pltpu.VMEM(STATE, f32), pltpu.VMEM(TILE, jnp.int32), pltpu.VMEM(TILE, jnp.int32)),
        in_specs=[hbm] * 7,
        out_specs=[vmem] * 3,
        scratch_shapes=[
            pltpu.SMEM(slot_atom.shape, jnp.int32),
            pltpu.SMEM(slot_corner.shape, jnp.int32),
            pltpu.SMEM(atom_species.shape, jnp.int32),
            pltpu.SMEM(radius.shape, f32),
            pltpu.VMEM((1, pairs), f32),
            pltpu.VMEM((size_x * size_y, size_z), f32),
            pltpu.VMEM((kinds, pairs, 1, pairs), f32),
            pltpu.SemaphoreType.DMA((7,)),
        ],
        compiler_params=params,
    )(
        *(
            pltpu.with_memory_space_constraint(x, pltpu.HBM)
            for x in (
                slot_atom,
                slot_corner,
                atom_species,
                radius,
                density_matrix,
                potential.reshape(size_x * size_y, size_z),
                coulomb.transpose(1, 0, 2),
            )
        )
    )
    bands = projections[0].transpose(1, 0, 2)
    delta, stack = pl.pallas_call(
        prepare,
        out_shape=(
            pltpu.VMEM((shapes * CODES, 2 * LANES), f32),
            pltpu.VMEM((3 * LANES, bands.shape[2]), bf16),
        ),
        in_specs=[vmem] * 3,
        out_specs=[vmem] * 2,
        compiler_params=params,
        cost_estimate=pl.CostEstimate(flops=500000, bytes_accessed=500000, transcendentals=0),
    )(kind_of, delta_table.transpose(1, 0, 2), bands)
    for axis in (2, 1):
        pay = pl.pallas_call(
            functools.partial(merge, axis, dims[axis]),
            out_shape=pltpu.VMEM(STATE, f32),
            in_specs=[vmem] * 3,
            out_specs=vmem,
            compiler_params=params,
        )(*exchange(pay, dims, axis))
    dh, applied = pl.pallas_call(
        functools.partial(back, 0, dims[0]),
        out_shape=(jax.ShapeDtypeStruct(density_matrix.shape, f32), jax.ShapeDtypeStruct(bands.shape, f32)),
        in_specs=[vmem] * 6,
        out_specs=[vmem] * 2,
        compiler_params=params,
    )(*exchange(pay, dims, 0), delta, codes, stack)
    return dh, applied.transpose(1, 0, 2)[None]


def solution(mesh):
    return jax.shard_map(
        local,
        mesh=mesh,
        in_specs=(
            P("gx", "gy", "gz"),
            P(AXES, None),
            P(),
            P(),
            P(),
            P(),
            P(AXES, None),
            P(None, AXES, None),
            P(AXES),
            P(AXES, None, None, None),
        ),
        out_specs=(P(AXES, None), P(AXES, None, None, None)),
        check_vma=False,
    )
```

```python
import functools
import math

import jax
import jax.numpy as jnp
from jax import lax
from jax.experimental import pallas as pl
from jax.experimental.pallas import tpu as pltpu
from jax.sharding import PartitionSpec as P

BOX = 16
CODES = 8
LANES = 128
PART = LANES - 16
AXES = ("gx", "gy", "gz")
COLOURS = (3, 2, 2)
ORDER = {1: (0,), 2: (0, 1), 3: (0, 1, 2)}
HALF = (BOX - 1) / 2.0
VMEM_BYTES = 8 << 20
harmonic_scale = 0.5 / math.sqrt(3.0)
f32 = jnp.float32
bf16 = jnp.bfloat16
TILE = (CODES, LANES)
STATE = (2 * CODES, LANES)


def dot(a, b):
    return jnp.dot(a, b, preferred_element_type=f32)


def split(x):
    high = x.astype(bf16)
    return high, (x - high.astype(f32)).astype(bf16)


def lanes_of(shape):
    return lax.broadcasted_iota(jnp.int32, shape, len(shape) - 1)


def quotient(x, by):
    return jnp.floor((x + 0.5) * (1.0 / by))


def front(
    dims,
    cells_y,
    atom_hbm,
    corner_hbm,
    species_hbm,
    radius_hbm,
    density_hbm,
    potential_hbm,
    coulomb_hbm,
    pay_ref,
    kinds_ref,
    codes_ref,
    atom_ref,
    corner_ref,
    species_ref,
    radius_ref,
    density_ref,
    v_ref,
    c_ref,
    sems,
):
    _, ny, nz = dims
    slots = atom_ref.shape[1]
    cells, size_z = v_ref.shape
    pairs, kinds, _ = coulomb_hbm.shape
    def cut(source, target, chunks, sem):
        size = -(-source.shape[0] // chunks // 8) * 8
        for at in range(0, source.shape[0], size):
            part = slice(at, min(at + size, source.shape[0]))
            pltpu.make_async_copy(source.at[part], target.at[part], sem).start()
        return pltpu.make_async_copy(target, target, sem)

    v_copy = cut(potential_hbm, v_ref, 8, sems.at[5])
    sources = (atom_hbm, corner_hbm, species_hbm, radius_hbm, density_hbm)
    targets = (atom_ref, corner_ref, species_ref, radius_ref, density_ref)
    copies = [pltpu.make_async_copy(s, t, sems.at[i]) for i, (s, t) in enumerate(zip(sources, targets))]
    for copy in copies:
        copy.start()
    for k in range(kinds):
        pltpu.make_async_copy(coulomb_hbm.at[:, k : k + 1, :], c_ref.at[k], sems.at[6]).start()
    c_copy = pltpu.make_async_copy(c_ref, c_ref, sems.at[6])
    index_x, index_y, index_z = (lax.axis_index(a) for a in AXES)
    me = (index_x * ny + index_y) * nz + index_z
    row = lax.broadcasted_iota(jnp.int32, TILE, 0)
    lane = lanes_of(TILE)
    zero = jnp.zeros(TILE, f32)
    for copy in copies[:4]:
        copy.wait()

    zero_i = jnp.zeros(TILE, jnp.int32)
    kx, ky, kz, alive, kind_of = zero_i, zero_i, zero_i, zero, zero_i
    radius = jnp.ones(TILE, f32)
    codes = jnp.full(TILE, -1, jnp.int32)
    for s in range(slots):
        atom = atom_ref[0, s]
        kind = species_ref[atom]
        x, y, z = corner_ref[0, 0, s], corner_ref[1, 0, s], corner_ref[2, 0, s]
        code = (x >> 31 & 4) | (y >> 31 & 2) | (z >> 31 & 1)
        if s > 0:
            code = jnp.where((atom | x | y | z) == 0, -1, code)
        hit = row == code
        kx = jnp.where(hit, x, kx)
        ky = jnp.where(hit, y, ky)
        kz = jnp.where(hit, z, kz)
        radius = jnp.where(hit, radius_ref[kind], radius)
        kind_of = jnp.where(hit, kind, kind_of)
        alive = jnp.where(hit, 1.0, alive)
        codes = jnp.where(row == s, code, codes)
    kx, ky, kz = (k.astype(f32) for k in (kx, ky, kz))
    kinds_ref[...] = kind_of
    codes_ref[...] = codes

    inverse = 1.0 / radius
    line = (lane.astype(f32) - HALF) * inverse
    line = jnp.where(lane < BOX, jnp.exp(-line * line), 0.0)
    line = jnp.sum(line, axis=1, keepdims=True)
    norm = alive / (line * line * line)

    def over(x, width):
        return jnp.concatenate([x] * (width // LANES), axis=1)

    def axis_of(position, corner, width):
        offset = position - over(corner, width)
        inside = (offset >= 0.0) & (offset < BOX)
        return (offset - HALF) * over(inverse, width), inside

    cell = lanes_of((CODES, cells)).astype(f32)
    cell_x = quotient(cell, cells_y)
    u, in_x = axis_of(cell_x, kx, cells)
    v, in_y = axis_of(cell - cell_x * cells_y, ky, cells)
    e = jnp.where(in_x & in_y, jnp.exp(-(u * u + v * v)), 0.0)
    eu, ev = e * u, e * v
    weights = jnp.concatenate([e, eu, ev, eu * v, eu * u, ev * v], axis=0)
    w_high, w_low = split(weights)
    w, in_z = axis_of(lanes_of((CODES, size_z)).astype(f32), kz, size_z)
    g = jnp.where(in_z, jnp.exp(-w * w), 0.0)
    gw = g * w

    v_copy.wait()
    v_high, v_low = split(v_ref[...])
    both = dot(jnp.concatenate([w_high, w_low], axis=0), v_high)
    m = both[: 6 * CODES] + both[6 * CODES :] + dot(w_high, v_low)
    m0, mu, mv, muv, muu, mvv = (m[CODES * i : CODES * (i + 1)] for i in range(6))
    parts = [
        m0 * g,
        mu * g,
        mv * g,
        m0 * gw,
        muv * g,
        mv * gw,
        mu * gw,
        0.5 * (muu - mvv) * g,
        harmonic_scale * (2.0 * m0 * (gw * w) - (muu + mvv) * g),
    ]
    partial = zero
    for i, part in enumerate(parts):
        partial = jnp.where(lane == PART + i, jnp.sum(part, axis=1, keepdims=True), partial)
    partial = partial * norm

    copies[4].wait()
    c_copy.wait()
    rest = pairs - LANES
    total = jnp.sum(c_ref[species_ref[me], :, 0, :] * (2.0 * density_ref[...]), axis=1, keepdims=True)
    square = (pairs, LANES)
    shift = lax.broadcasted_iota(jnp.int32, square, 0) - lanes_of(square)
    head = jnp.sum(jnp.where(shift == 0, total, 0.0), axis=0, keepdims=True)
    tail = jnp.sum(jnp.where(shift == LANES, total, 0.0), axis=0, keepdims=True)
    pay_ref[:CODES] = jnp.where(row == 0, head, 0.0)
    pay_ref[CODES:] = jnp.where(lane < PART, jnp.where(row == 0, tail, 0.0), partial)


def prepare(kinds_ref, delta_ref, projections_ref, out_ref, stack_ref):
    shapes, kinds, pairs = delta_ref.shape
    projectors, slots, bands = projections_ref.shape
    out_ref[:, LANES:] = jnp.zeros((shapes * CODES, LANES), f32)
    kind = jnp.concatenate([kinds_ref[...]] * 2, axis=1)[:, :pairs]
    for i in range(shapes):
        rows = delta_ref[i]
        chosen = jnp.zeros((CODES, pairs), f32)
        for k in range(kinds):
            chosen = jnp.where(kind == k, rows[k : k + 1], chosen)
        out_ref[i * CODES : (i + 1) * CODES, :pairs] = chosen
    stack = projections_ref[...].reshape(projectors * slots, bands)
    stack = jnp.concatenate([stack, jnp.zeros((LANES - projectors * slots, bands), f32)], axis=0)
    high, low = split(stack)
    for at, part in enumerate((high, high, low)):
        stack_ref[at * LANES : (at + 1) * LANES] = part


def merged(axis, size, pay_ref, *got_refs):
    index = lax.axis_index(AXES[axis])
    got_refs = got_refs[::-1]
    colours = len(got_refs)
    step = CODES // 2 >> axis
    row = lax.broadcasted_iota(jnp.int32, TILE, 0)
    higher = row // step % 2 == 1
    partial = lanes_of(TILE) >= PART
    add_up = partial & (index < size - 1)

    def of_link(link, rows):
        got = [ref[rows] for ref in got_refs]
        chosen = got[0]
        for colour in range(1, colours):
            chosen = jnp.where(link % colours == colour, got[colour], chosen)
        return chosen

    first, last = slice(0, CODES), slice(CODES, 2 * CODES)
    below = index + colours - 1
    down = [pltpu.roll(of_link(below, rows), step, 0) for rows in (first, last)]
    up = pltpu.roll(of_link(index, last), CODES - step, 0)
    x = pay_ref[last]
    kept = jnp.where(add_up, x + up, x)
    taken = jnp.where(partial, x + down[1], down[1])
    return jnp.where(higher, down[0], pay_ref[first]), jnp.where(higher, taken, kept)


def merge(axis, size, *refs):
    out_ref = refs[-1]
    out_ref[:CODES], out_ref[CODES:] = merged(axis, size, *refs[:-1])


def back(axis, size, *refs):
    *states, delta_ref, codes_ref, stack_ref, dh_ref, applied_ref = refs
    projectors, slots, _ = applied_ref.shape
    pairs = dh_ref.shape[1]
    width = 2 * LANES
    head, tail = merged(axis, size, *states)
    h = jnp.concatenate([head, jnp.where(lanes_of(TILE) < PART, tail, 0.0)], axis=1)
    for i in range(delta_ref.shape[0] // CODES):
        total = tail[:, PART + i : PART + i + 1]
        h = h + jnp.broadcast_to(total, (CODES, width)) * delta_ref[i * CODES : (i + 1) * CODES]
    dh_ref[...] = h[:1, :pairs]
    codes = codes_ref[...]
    at = jnp.maximum(codes, 0)
    by_slot = [jnp.where(codes < 0, 0.0, jnp.take_along_axis(half, at, axis=0)) for half in (h[:, :LANES], h[:, LANES:])]
    lane = lanes_of(TILE)
    diagonal = lane % slots == lax.broadcasted_iota(jnp.int32, TILE, 0)
    rows = []
    for j in range(projectors):
        pair = lane // slots * projectors + j
        chosen = jnp.take_along_axis(by_slot[0], pair % LANES, axis=1)
        chosen = jnp.where(pair < LANES, chosen, jnp.take_along_axis(by_slot[1], pair % LANES, axis=1))
        rows.append(jnp.where(diagonal & (lane < projectors * slots), chosen, 0.0))
    if projectors % 2:
        rows.append(jnp.zeros(TILE, f32))
    high, low = split(jnp.concatenate(rows, axis=0))
    out = dot(jnp.concatenate([high, low, high], axis=1), stack_ref[...])
    applied_ref[...] = out[: projectors * slots].reshape(applied_ref.shape)


def swaps(dims, axis, colour, colours):
    nx, ny, nz = dims
    size = dims[axis]

    def partner(at):
        i = at[axis]
        for other in (i + 1, i - 1):
            if 0 <= other < size and min(i, other) % colours == colour:
                return at[:axis] + (other,) + at[axis + 1 :]
        if axis == 0 and at[1] ^ 1 < ny:
            return (at[0], at[1] ^ 1, at[2])
        if axis == 1 and colours == 2 and size % 2 == 0:
            return (at[0], size - 1 - i, at[2])
        return at

    def line(at):
        return (at[0] * ny + at[1]) * nz + at[2]

    every = [(x, y, z) for x in range(nx) for y in range(ny) for z in range(nz)]
    return [(line(at), line(partner(at))) for at in every]


def exchange(x, dims, axis):
    colours = COLOURS[axis] if dims[axis] > 2 else 1
    got = {c: lax.ppermute(x, AXES, swaps(dims, axis, c, colours)) for c in ORDER[colours]}
    return [x] + [got[c] for c in reversed(range(colours))]


def local(
    potential,
    density_matrix,
    delta_table,
    coulomb,
    radius,
    atom_species,
    slot_atom,
    slot_corner,
    slot_count,
    projections,
):
    dims = tuple(lax.axis_size(a) for a in AXES)
    slots = slot_atom.shape[1]
    assert density_matrix.shape[0] == 1 and slots == CODES
    size_x, size_y, size_z = potential.shape
    pairs = density_matrix.shape[1]
    kinds, shapes, _ = delta_table.shape
    vmem, hbm = (pl.BlockSpec(memory_space=m) for m in (pltpu.VMEM, pltpu.HBM))
    params = pltpu.CompilerParams(vmem_limit_bytes=VMEM_BYTES)
    pay, kind_of, codes = pl.pallas_call(
        functools.partial(front, dims, size_y),
        out_shape=(pltpu.VMEM(STATE, f32), pltpu.VMEM(TILE, jnp.int32), pltpu.VMEM(TILE, jnp.int32)),
        in_specs=[hbm] * 7,
        out_specs=[vmem] * 3,
        scratch_shapes=[
            pltpu.SMEM(slot_atom.shape, jnp.int32),
            pltpu.SMEM(slot_corner.shape, jnp.int32),
            pltpu.SMEM(atom_species.shape, jnp.int32),
            pltpu.SMEM(radius.shape, f32),
            pltpu.VMEM((1, pairs), f32),
            pltpu.VMEM((size_x * size_y, size_z), f32),
            pltpu.VMEM((kinds, pairs, 1, pairs), f32),
            pltpu.SemaphoreType.DMA((7,)),
        ],
        compiler_params=params,
    )(
        *(
            pltpu.with_memory_space_constraint(x, pltpu.HBM)
            for x in (
                slot_atom,
                slot_corner,
                atom_species,
                radius,
                density_matrix,
                potential.reshape(size_x * size_y, size_z),
                coulomb.transpose(1, 0, 2),
            )
        )
    )
    bands = projections[0].transpose(1, 0, 2)
    delta, stack = pl.pallas_call(
        prepare,
        out_shape=(
            pltpu.VMEM((shapes * CODES, 2 * LANES), f32),
            pltpu.VMEM((3 * LANES, bands.shape[2]), bf16),
        ),
        in_specs=[vmem] * 3,
        out_specs=[vmem] * 2,
        compiler_params=params,
        cost_estimate=pl.CostEstimate(flops=500000, bytes_accessed=500000, transcendentals=0),
    )(kind_of, delta_table.transpose(1, 0, 2), bands)
    for axis in (2, 1):
        pay = pl.pallas_call(
            functools.partial(merge, axis, dims[axis]),
            out_shape=pltpu.VMEM(STATE, f32),
            out_specs=vmem,
            compiler_params=params,
        )(*exchange(pay, dims, axis))
    dh, applied = pl.pallas_call(
        functools.partial(back, 0, dims[0]),
        out_shape=(jax.ShapeDtypeStruct(density_matrix.shape, f32), jax.ShapeDtypeStruct(bands.shape, f32)),
        out_specs=[vmem] * 2,
        compiler_params=params,
    )(*exchange(pay, dims, 0), delta, codes, stack)
    return dh, applied.transpose(1, 0, 2)[None]


def solution(mesh):
    return jax.shard_map(
        local,
        mesh=mesh,
        in_specs=(
            P("gx", "gy", "gz"),
            P(AXES, None),
            P(),
            P(),
            P(),
            P(),
            P(AXES, None),
            P(None, AXES, None),
            P(AXES),
            P(AXES, None, None, None),
        ),
        out_specs=(P(AXES, None), P(AXES, None, None, None)),
        check_vma=False,
    )
```

```python
import functools
import math

import jax
import jax.numpy as jnp
from jax import lax
from jax.experimental import pallas as pl
from jax.experimental.pallas import tpu as pltpu
from jax.sharding import PartitionSpec as P

BOX = 16
CODES = 8
LANES = 128
PART = LANES - 16
AXES = ("gx", "gy", "gz")
COLOURS = (3, 2, 2)
HALF = (BOX - 1) / 2.0
VMEM_BYTES = 8 << 20
harmonic_scale = 0.5 / math.sqrt(3.0)
f32 = jnp.float32
bf16 = jnp.bfloat16
TILE = (CODES, LANES)
STATE = (2 * CODES, LANES)


def dot(a, b):
    return jnp.dot(a, b, preferred_element_type=f32)


def split(x):
    high = x.astype(bf16)
    return high, (x - high.astype(f32)).astype(bf16)


def lanes_of(shape):
    return lax.broadcasted_iota(jnp.int32, shape, len(shape) - 1)


def quotient(x, by):
    return jnp.floor((x + 0.5) * (1.0 / by))


def front(
    dims,
    cells_y,
    atom_hbm,
    corner_hbm,
    species_hbm,
    radius_hbm,
    density_hbm,
    potential_hbm,
    coulomb_hbm,
    pay_ref,
    kinds_ref,
    codes_ref,
    atom_ref,
    corner_ref,
    species_ref,
    radius_ref,
    density_ref,
    v_ref,
    c_ref,
    sems,
):
    _, ny, nz = dims
    slots = atom_ref.shape[1]
    cells, size_z = v_ref.shape
    pairs, kinds, _ = coulomb_hbm.shape

    def cut(source, target, chunks, sem):
        size = -(-source.shape[0] // chunks // 8) * 8
        for at in range(0, source.shape[0], size):
            part = slice(at, min(at + size, source.shape[0]))
            pltpu.make_async_copy(source.at[part], target.at[part], sem).start()
        return pltpu.make_async_copy(target, target, sem)

    v_copy = cut(potential_hbm, v_ref, 8, sems.at[5])
    sources = (atom_hbm, corner_hbm, species_hbm, radius_hbm, density_hbm)
    targets = (atom_ref, corner_ref, species_ref, radius_ref, density_ref)
    copies = [pltpu.make_async_copy(s, t, sems.at[i]) for i, (s, t) in enumerate(zip(sources, targets))]
    for copy in copies:
        copy.start()
    for k in range(kinds):
        pltpu.make_async_copy(coulomb_hbm.at[:, k : k + 1, :], c_ref.at[k], sems.at[6]).start()
    c_copy = pltpu.make_async_copy(c_ref, c_ref, sems.at[6])
    index_x, index_y, index_z = (lax.axis_index(a) for a in AXES)
    me = (index_x * ny + index_y) * nz + index_z
    row = lax.broadcasted_iota(jnp.int32, TILE, 0)
    lane = lanes_of(TILE)
    zero = jnp.zeros(TILE, f32)
    for copy in copies[:4]:
        copy.wait()

    zero_i = jnp.zeros(TILE, jnp.int32)
    kx, ky, kz, alive, kind_of = zero_i, zero_i, zero_i, zero, zero_i
    radius = jnp.ones(TILE, f32)
    codes = jnp.full(TILE, -1, jnp.int32)
    for s in range(slots):
        atom = atom_ref[0, s]
        kind = species_ref[atom]
        x, y, z = corner_ref[0, 0, s], corner_ref[1, 0, s], corner_ref[2, 0, s]
        code = (x >> 31 & 4) | (y >> 31 & 2) | (z >> 31 & 1)
        if s > 0:
            code = jnp.where((atom | x | y | z) == 0, -1, code)
        hit = row == code
        kx = jnp.where(hit, x, kx)
        ky = jnp.where(hit, y, ky)
        kz = jnp.where(hit, z, kz)
        radius = jnp.where(hit, radius_ref[kind], radius)
        kind_of = jnp.where(hit, kind, kind_of)
        alive = jnp.where(hit, 1.0, alive)
        codes = jnp.where(row == s, code, codes)
    kx, ky, kz = (k.astype(f32) for k in (kx, ky, kz))
    kinds_ref[...] = kind_of
    codes_ref[...] = codes

    inverse = 1.0 / radius
    line = (lane.astype(f32) - HALF) * inverse
    line = jnp.where(lane < BOX, jnp.exp(-line * line), 0.0)
    line = jnp.sum(line, axis=1, keepdims=True)
    norm = alive / (line * line * line)

    def over(x, width):
        return jnp.concatenate([x] * (width // LANES), axis=1)

    def axis_of(position, corner, width):
        offset = position - over(corner, width)
        inside = (offset >= 0.0) & (offset < BOX)
        return (offset - HALF) * over(inverse, width), inside

    cell = lanes_of((CODES, cells)).astype(f32)
    cell_x = quotient(cell, cells_y)
    u, in_x = axis_of(cell_x, kx, cells)
    v, in_y = axis_of(cell - cell_x * cells_y, ky, cells)
    e = jnp.where(in_x & in_y, jnp.exp(-(u * u + v * v)), 0.0)
    eu, ev = e * u, e * v
    weights = jnp.concatenate([e, eu, ev, eu * v, eu * u, ev * v], axis=0)
    w_high, w_low = split(weights)
    w, in_z = axis_of(lanes_of((CODES, size_z)).astype(f32), kz, size_z)
    g = jnp.where(in_z, jnp.exp(-w * w), 0.0)
    gw = g * w

    v_copy.wait()
    v_high, v_low = split(v_ref[...])
    both = dot(jnp.concatenate([w_high, w_low], axis=0), v_high)
    m = both[: 6 * CODES] + both[6 * CODES :] + dot(w_high, v_low)
    m0, mu, mv, muv, muu, mvv = (m[CODES * i : CODES * (i + 1)] for i in range(6))
    parts = [
        m0 * g,
        mu * g,
        mv * g,
        m0 * gw,
        muv * g,
        mv * gw,
        mu * gw,
        0.5 * (muu - mvv) * g,
        harmonic_scale * (2.0 * m0 * (gw * w) - (muu + mvv) * g),
    ]
    partial = zero
    for i, part in enumerate(parts):
        partial = jnp.where(lane == PART + i, jnp.sum(part, axis=1, keepdims=True), partial)
    partial = partial * norm

    copies[4].wait()
    c_copy.wait()
    rest = pairs - LANES
    total = jnp.sum(c_ref[species_ref[me], :, 0, :] * (2.0 * density_ref[...]), axis=1, keepdims=True)
    square = (pairs, LANES)
    shift = lax.broadcasted_iota(jnp.int32, square, 0) - lanes_of(square)
    head = jnp.sum(jnp.where(shift == 0, total, 0.0), axis=0, keepdims=True)
    tail = jnp.sum(jnp.where(shift == LANES, total, 0.0), axis=0, keepdims=True)
    pay_ref[:CODES] = jnp.where(row == 0, head, 0.0)
    pay_ref[CODES:] = jnp.where(lane < PART, jnp.where(row == 0, tail, 0.0), partial)


def prepare(kinds_ref, delta_ref, projections_ref, out_ref, stack_ref):
    shapes, kinds, pairs = delta_ref.shape
    projectors, slots, bands = projections_ref.shape
    out_ref[:, LANES:] = jnp.zeros((shapes * CODES, LANES), f32)
    kind = jnp.concatenate([kinds_ref[...]] * 2, axis=1)[:, :pairs]
    for i in range(shapes):
        rows = delta_ref[i]
        chosen = jnp.zeros((CODES, pairs), f32)
        for k in range(kinds):
            chosen = jnp.where(kind == k, rows[k : k + 1], chosen)
        out_ref[i * CODES : (i + 1) * CODES, :pairs] = chosen
    stack = projections_ref[...].reshape(projectors * slots, bands)
    stack = jnp.concatenate([stack, jnp.zeros((LANES - projectors * slots, bands), f32)], axis=0)
    high, low = split(stack)
    for at, part in enumerate((high, high, low)):
        stack_ref[at * LANES : (at + 1) * LANES] = part


def merged(axis, size, pay_ref, *got_refs):
    index = lax.axis_index(AXES[axis])
    got_refs = got_refs[::-1]
    colours = len(got_refs)
    step = CODES // 2 >> axis
    row = lax.broadcasted_iota(jnp.int32, TILE, 0)
    higher = row // step % 2 == 1
    partial = lanes_of(TILE) >= PART
    add_up = partial & (index < size - 1)

    def of_link(link, rows):
        got = [ref[rows] for ref in got_refs]
        chosen = got[0]
        for colour in range(1, colours):
            chosen = jnp.where(link % colours == colour, got[colour], chosen)
        return chosen

    first, last = slice(0, CODES), slice(CODES, 2 * CODES)
    below = index + colours - 1
    down = [pltpu.roll(of_link(below, rows), step, 0) for rows in (first, last)]
    up = pltpu.roll(of_link(index, last), CODES - step, 0)
    x = pay_ref[last]
    kept = jnp.where(add_up, x + up, x)
    taken = jnp.where(partial, x + down[1], down[1])
    return jnp.where(higher, down[0], pay_ref[first]), jnp.where(higher, taken, kept)


def merge(axis, size, *refs):
    out_ref = refs[-1]
    out_ref[:CODES], out_ref[CODES:] = merged(axis, size, *refs[:-1])


def back(axis, size, *refs):
    *states, delta_ref, codes_ref, stack_ref, dh_ref, applied_ref = refs
    projectors, slots, _ = applied_ref.shape
    pairs = dh_ref.shape[1]
    width = 2 * LANES
    head, tail = merged(axis, size, *states)
    h = jnp.concatenate([head, jnp.where(lanes_of(TILE) < PART, tail, 0.0)], axis=1)
    for i in range(delta_ref.shape[0] // CODES):
        total = tail[:, PART + i : PART + i + 1]
        h = h + jnp.broadcast_to(total, (CODES, width)) * delta_ref[i * CODES : (i + 1) * CODES]
    dh_ref[...] = h[:1, :pairs]
    codes = codes_ref[...]
    at = jnp.maximum(codes, 0)
    by_slot = [jnp.where(codes < 0, 0.0, jnp.take_along_axis(half, at, axis=0)) for half in (h[:, :LANES], h[:, LANES:])]
    lane = lanes_of(TILE)
    diagonal = lane % slots == lax.broadcasted_iota(jnp.int32, TILE, 0)
    rows = []
    for j in range(projectors):
        pair = lane // slots * projectors + j
        chosen = jnp.take_along_axis(by_slot[0], pair % LANES, axis=1)
        chosen = jnp.where(pair < LANES, chosen, jnp.take_along_axis(by_slot[1], pair % LANES, axis=1))
        rows.append(jnp.where(diagonal & (lane < projectors * slots), chosen, 0.0))
    if projectors % 2:
        rows.append(jnp.zeros(TILE, f32))
    high, low = split(jnp.concatenate(rows, axis=0))
    out = dot(jnp.concatenate([high, low, high], axis=1), stack_ref[...])
    applied_ref[...] = out[: projectors * slots].reshape(applied_ref.shape)


def swaps(dims, axis, colour, colours):
    nx, ny, nz = dims
    size = dims[axis]

    def partner(at):
        i = at[axis]
        for other in (i + 1, i - 1):
            if 0 <= other < size and min(i, other) % colours == colour:
                return at[:axis] + (other,) + at[axis + 1 :]
        if axis == 0 and at[1] ^ 1 < ny:
            return (at[0], at[1] ^ 1, at[2])
        if axis == 1 and colours == 2 and size % 2 == 0:
            return (at[0], size - 1 - i, at[2])
        return at

    def line(at):
        return (at[0] * ny + at[1]) * nz + at[2]

    every = [(x, y, z) for x in range(nx) for y in range(ny) for z in range(nz)]
    return [(line(at), line(partner(at))) for at in every]


def exchange(x, dims, axis):
    colours = COLOURS[axis] if dims[axis] > 2 else 1
    got = [lax.ppermute(x, AXES, swaps(dims, axis, c, colours)) for c in range(colours)]
    return [x] + got[::-1]


def local(
    potential,
    density_matrix,
    delta_table,
    coulomb,
    radius,
    atom_species,
    slot_atom,
    slot_corner,
    slot_count,
    projections,
):
    dims = tuple(lax.axis_size(a) for a in AXES)
    slots = slot_atom.shape[1]
    assert density_matrix.shape[0] == 1 and slots == CODES
    size_x, size_y, size_z = potential.shape
    pairs = density_matrix.shape[1]
    kinds, shapes, _ = delta_table.shape
    vmem, hbm = (pl.BlockSpec(memory_space=m) for m in (pltpu.VMEM, pltpu.HBM))
    params = pltpu.CompilerParams(vmem_limit_bytes=VMEM_BYTES)
    pay, kind_of, codes = pl.pallas_call(
        functools.partial(front, dims, size_y),
        out_shape=(pltpu.VMEM(STATE, f32), pltpu.VMEM(TILE, jnp.int32), pltpu.VMEM(TILE, jnp.int32)),
        in_specs=[hbm] * 7,
        out_specs=[vmem] * 3,
        scratch_shapes=[
            pltpu.SMEM(slot_atom.shape, jnp.int32),
            pltpu.SMEM(slot_corner.shape, jnp.int32),
            pltpu.SMEM(atom_species.shape, jnp.int32),
            pltpu.SMEM(radius.shape, f32),
            pltpu.VMEM((1, pairs), f32),
            pltpu.VMEM((size_x * size_y, size_z), f32),
            pltpu.VMEM((kinds, pairs, 1, pairs), f32),
            pltpu.SemaphoreType.DMA((7,)),
        ],
        compiler_params=params,
    )(
        *(
            pltpu.with_memory_space_constraint(x, pltpu.HBM)
            for x in (
                slot_atom,
                slot_corner,
                atom_species,
                radius,
                density_matrix,
                potential.reshape(size_x * size_y, size_z),
                coulomb.transpose(1, 0, 2),
            )
        )
    )
    bands = projections[0].transpose(1, 0, 2)
    delta, stack = pl.pallas_call(
        prepare,
        out_shape=(
            pltpu.VMEM((shapes * CODES, 2 * LANES), f32),
            pltpu.VMEM((3 * LANES, bands.shape[2]), bf16),
        ),
        in_specs=[vmem] * 3,
        out_specs=[vmem] * 2,
        compiler_params=params,
        cost_estimate=pl.CostEstimate(flops=500000, bytes_accessed=500000, transcendentals=0),
    )(kind_of, delta_table.transpose(1, 0, 2), bands)
    for axis in (1, 2):
        pay = pl.pallas_call(
            functools.partial(merge, axis, dims[axis]),
            out_shape=pltpu.VMEM(STATE, f32),
            out_specs=vmem,
            compiler_params=params,
        )(*exchange(pay, dims, axis))
    dh, applied = pl.pallas_call(
        functools.partial(back, 0, dims[0]),
        out_shape=(jax.ShapeDtypeStruct(density_matrix.shape, f32), jax.ShapeDtypeStruct(bands.shape, f32)),
        out_specs=[vmem] * 2,
        compiler_params=params,
    )(*exchange(pay, dims, 0), delta, codes, stack)
    return dh, applied.transpose(1, 0, 2)[None]


def solution(mesh):
    return jax.shard_map(
        local,
        mesh=mesh,
        in_specs=(
            P("gx", "gy", "gz"),
            P(AXES, None),
            P(),
            P(),
            P(),
            P(),
            P(AXES, None),
            P(None, AXES, None),
            P(AXES),
            P(AXES, None, None, None),
        ),
        out_specs=(P(AXES, None), P(AXES, None, None, None)),
        check_vma=False,
    )
```

```python
import functools
import math

import jax
import jax.numpy as jnp
from jax import lax
from jax.experimental import pallas as pl
from jax.experimental.pallas import tpu as pltpu
from jax.sharding import PartitionSpec as P

BOX = 16
CODES = 8
LANES = 128
PART = LANES - 16
AXES = ("gx", "gy", "gz")
COLOURS = (3, 2, 2)
ORDER = {1: (0,), 2: (0, 1), 3: (0, 1, 2)}
HALF = (BOX - 1) / 2.0
VMEM_BYTES = 8 << 20
harmonic_scale = 0.5 / math.sqrt(3.0)
f32 = jnp.float32
bf16 = jnp.bfloat16
TILE = (CODES, LANES)
STATE = (2 * CODES, LANES)


def dot(a, b):
    return jnp.dot(a, b, preferred_element_type=f32)


def split(x):
    high = x.astype(bf16)
    return high, (x - high.astype(f32)).astype(bf16)


def lanes_of(shape):
    return lax.broadcasted_iota(jnp.int32, shape, len(shape) - 1)


def quotient(x, by):
    return jnp.floor((x + 0.5) * (1.0 / by))


def front(
    dims,
    cells_y,
    atom_hbm,
    corner_hbm,
    species_hbm,
    radius_hbm,
    density_hbm,
    potential_hbm,
    coulomb_hbm,
    pay_ref,
    kinds_ref,
    codes_ref,
    atom_ref,
    corner_ref,
    species_ref,
    radius_ref,
    density_ref,
    v_ref,
    c_ref,
    sems,
):
    _, ny, nz = dims
    slots = atom_ref.shape[1]
    cells, size_z = v_ref.shape
    pairs, kinds, _ = coulomb_hbm.shape
    def cut(source, target, chunks, sem):
        size = -(-source.shape[0] // chunks // 8) * 8
        for at in range(0, source.shape[0], size):
            part = slice(at, min(at + size, source.shape[0]))
            pltpu.make_async_copy(source.at[part], target.at[part], sem).start()
        return pltpu.make_async_copy(target, target, sem)

    v_copy = cut(potential_hbm, v_ref, 1, sems.at[5])
    sources = (atom_hbm, corner_hbm, species_hbm, radius_hbm, density_hbm)
    targets = (atom_ref, corner_ref, species_ref, radius_ref, density_ref)
    copies = [pltpu.make_async_copy(s, t, sems.at[i]) for i, (s, t) in enumerate(zip(sources, targets))]
    for copy in copies:
        copy.start()
    for k in range(kinds):
        pltpu.make_async_copy(coulomb_hbm.at[:, k : k + 1, :], c_ref.at[k], sems.at[6]).start()
    c_copy = pltpu.make_async_copy(c_ref, c_ref, sems.at[6])
    index_x, index_y, index_z = (lax.axis_index(a) for a in AXES)
    me = (index_x * ny + index_y) * nz + index_z
    row = lax.broadcasted_iota(jnp.int32, TILE, 0)
    lane = lanes_of(TILE)
    zero = jnp.zeros(TILE, f32)
    for copy in copies[:4]:
        copy.wait()

    zero_i = jnp.zeros(TILE, jnp.int32)
    kx, ky, kz, alive, kind_of = zero_i, zero_i, zero_i, zero, zero_i
    radius = jnp.ones(TILE, f32)
    codes = jnp.full(TILE, -1, jnp.int32)
    for s in range(slots):
        atom = atom_ref[0, s]
        kind = species_ref[atom]
        x, y, z = corner_ref[0, 0, s], corner_ref[1, 0, s], corner_ref[2, 0, s]
        code = (x >> 31 & 4) | (y >> 31 & 2) | (z >> 31 & 1)
        if s > 0:
            code = jnp.where((atom | x | y | z) == 0, -1, code)
        hit = row == code
        kx = jnp.where(hit, x, kx)
        ky = jnp.where(hit, y, ky)
        kz = jnp.where(hit, z, kz)
        radius = jnp.where(hit, radius_ref[kind], radius)
        kind_of = jnp.where(hit, kind, kind_of)
        alive = jnp.where(hit, 1.0, alive)
        codes = jnp.where(row == s, code, codes)
    kx, ky, kz = (k.astype(f32) for k in (kx, ky, kz))
    kinds_ref[...] = kind_of
    codes_ref[...] = codes

    inverse = 1.0 / radius
    line = (lane.astype(f32) - HALF) * inverse
    line = jnp.where(lane < BOX, jnp.exp(-line * line), 0.0)
    line = jnp.sum(line, axis=1, keepdims=True)
    norm = alive / (line * line * line)

    def over(x, width):
        return jnp.concatenate([x] * (width // LANES), axis=1)

    def axis_of(position, corner, width):
        offset = position - over(corner, width)
        inside = (offset >= 0.0) & (offset < BOX)
        return (offset - HALF) * over(inverse, width), inside

    cell = lanes_of((CODES, cells)).astype(f32)
    cell_x = quotient(cell, cells_y)
    u, in_x = axis_of(cell_x, kx, cells)
    v, in_y = axis_of(cell - cell_x * cells_y, ky, cells)
    e = jnp.where(in_x & in_y, jnp.exp(-(u * u + v * v)), 0.0)
    eu, ev = e * u, e * v
    weights = jnp.concatenate([e, eu, ev, eu * v, eu * u, ev * v], axis=0)
    w_high, w_low = split(weights)
    w, in_z = axis_of(lanes_of((CODES, size_z)).astype(f32), kz, size_z)
    g = jnp.where(in_z, jnp.exp(-w * w), 0.0)
    gw = g * w

    v_copy.wait()
    v_high, v_low = split(v_ref[...])
    both = dot(jnp.concatenate([w_high, w_low], axis=0), v_high)
    m = both[: 6 * CODES] + both[6 * CODES :] + dot(w_high, v_low)
    m0, mu, mv, muv, muu, mvv = (m[CODES * i : CODES * (i + 1)] for i in range(6))
    parts = [
        m0 * g,
        mu * g,
        mv * g,
        m0 * gw,
        muv * g,
        mv * gw,
        mu * gw,
        0.5 * (muu - mvv) * g,
        harmonic_scale * (2.0 * m0 * (gw * w) - (muu + mvv) * g),
    ]
    partial = zero
    for i, part in enumerate(parts):
        partial = jnp.where(lane == PART + i, jnp.sum(part, axis=1, keepdims=True), partial)
    partial = partial * norm

    copies[4].wait()
    c_copy.wait()
    rest = pairs - LANES
    total = jnp.sum(c_ref[species_ref[me], :, 0, :] * (2.0 * density_ref[...]), axis=1, keepdims=True)
    square = (pairs, LANES)
    shift = lax.broadcasted_iota(jnp.int32, square, 0) - lanes_of(square)
    head = jnp.sum(jnp.where(shift == 0, total, 0.0), axis=0, keepdims=True)
    tail = jnp.sum(jnp.where(shift == LANES, total, 0.0), axis=0, keepdims=True)
    pay_ref[:CODES] = jnp.where(row == 0, head, 0.0)
    pay_ref[CODES:] = jnp.where(lane < PART, jnp.where(row == 0, tail, 0.0), partial)


def prepare(kinds_ref, delta_ref, projections_ref, out_ref, stack_ref):
    shapes, kinds, pairs = delta_ref.shape
    projectors, slots, bands = projections_ref.shape
    out_ref[:, LANES:] = jnp.zeros((shapes * CODES, LANES), f32)
    kind = jnp.concatenate([kinds_ref[...]] * 2, axis=1)[:, :pairs]
    for i in range(shapes):
        rows = delta_ref[i]
        chosen = jnp.zeros((CODES, pairs), f32)
        for k in range(kinds):
            chosen = jnp.where(kind == k, rows[k : k + 1], chosen)
        out_ref[i * CODES : (i + 1) * CODES, :pairs] = chosen
    stack = projections_ref[...].reshape(projectors * slots, bands)
    stack = jnp.concatenate([stack, jnp.zeros((LANES - projectors * slots, bands), f32)], axis=0)
    high, low = split(stack)
    for at, part in enumerate((high, high, low)):
        stack_ref[at * LANES : (at + 1) * LANES] = part


def merged(axis, size, pay_ref, *got_refs):
    index = lax.axis_index(AXES[axis])
    got_refs = got_refs[::-1]
    colours = len(got_refs)
    step = CODES // 2 >> axis
    row = lax.broadcasted_iota(jnp.int32, TILE, 0)
    higher = row // step % 2 == 1
    partial = lanes_of(TILE) >= PART
    add_up = partial & (index < size - 1)

    def of_link(link, rows):
        got = [ref[rows] for ref in got_refs]
        chosen = got[0]
        for colour in range(1, colours):
            chosen = jnp.where(link % colours == colour, got[colour], chosen)
        return chosen

    first, last = slice(0, CODES), slice(CODES, 2 * CODES)
    below = index + colours - 1
    down = [pltpu.roll(of_link(below, rows), step, 0) for rows in (first, last)]
    up = pltpu.roll(of_link(index, last), CODES - step, 0)
    x = pay_ref[last]
    kept = jnp.where(add_up, x + up, x)
    taken = jnp.where(partial, x + down[1], down[1])
    return jnp.where(higher, down[0], pay_ref[first]), jnp.where(higher, taken, kept)


def merge(axis, size, *refs):
    out_ref = refs[-1]
    out_ref[:CODES], out_ref[CODES:] = merged(axis, size, *refs[:-1])


def back(axis, size, *refs):
    *states, delta_ref, codes_ref, stack_ref, dh_ref, applied_ref = refs
    projectors, slots, _ = applied_ref.shape
    pairs = dh_ref.shape[1]
    width = 2 * LANES
    head, tail = merged(axis, size, *states)
    h = jnp.concatenate([head, jnp.where(lanes_of(TILE) < PART, tail, 0.0)], axis=1)
    for i in range(delta_ref.shape[0] // CODES):
        total = tail[:, PART + i : PART + i + 1]
        h = h + jnp.broadcast_to(total, (CODES, width)) * delta_ref[i * CODES : (i + 1) * CODES]
    dh_ref[...] = h[:1, :pairs]
    codes = codes_ref[...]
    at = jnp.maximum(codes, 0)
    by_slot = [jnp.where(codes < 0, 0.0, jnp.take_along_axis(half, at, axis=0)) for half in (h[:, :LANES], h[:, LANES:])]
    lane = lanes_of(TILE)
    diagonal = lane % slots == lax.broadcasted_iota(jnp.int32, TILE, 0)
    rows = []
    for j in range(projectors):
        pair = lane // slots * projectors + j
        chosen = jnp.take_along_axis(by_slot[0], pair % LANES, axis=1)
        chosen = jnp.where(pair < LANES, chosen, jnp.take_along_axis(by_slot[1], pair % LANES, axis=1))
        rows.append(jnp.where(diagonal & (lane < projectors * slots), chosen, 0.0))
    if projectors % 2:
        rows.append(jnp.zeros(TILE, f32))
    high, low = split(jnp.concatenate(rows, axis=0))
    out = dot(jnp.concatenate([high, low, high], axis=1), stack_ref[...])
    applied_ref[...] = out[: projectors * slots].reshape(applied_ref.shape)


def swaps(dims, axis, colour, colours):
    nx, ny, nz = dims
    size = dims[axis]

    def partner(at):
        i = at[axis]
        for other in (i + 1, i - 1):
            if 0 <= other < size and min(i, other) % colours == colour:
                return at[:axis] + (other,) + at[axis + 1 :]
        if axis == 0 and at[1] ^ 1 < ny:
            return (at[0], at[1] ^ 1, at[2])
        if axis == 1 and colours == 2 and size % 2 == 0:
            return (at[0], size - 1 - i, at[2])
        return at

    def line(at):
        return (at[0] * ny + at[1]) * nz + at[2]

    every = [(x, y, z) for x in range(nx) for y in range(ny) for z in range(nz)]
    return [(line(at), line(partner(at))) for at in every]


def exchange(x, dims, axis):
    colours = COLOURS[axis] if dims[axis] > 2 else 1
    got = {c: lax.ppermute(x, AXES, swaps(dims, axis, c, colours)) for c in ORDER[colours]}
    return [x] + [got[c] for c in reversed(range(colours))]


def local(
    potential,
    density_matrix,
    delta_table,
    coulomb,
    radius,
    atom_species,
    slot_atom,
    slot_corner,
    slot_count,
    projections,
):
    dims = tuple(lax.axis_size(a) for a in AXES)
    slots = slot_atom.shape[1]
    assert density_matrix.shape[0] == 1 and slots == CODES
    size_x, size_y, size_z = potential.shape
    pairs = density_matrix.shape[1]
    kinds, shapes, _ = delta_table.shape
    vmem, hbm = (pl.BlockSpec(memory_space=m) for m in (pltpu.VMEM, pltpu.HBM))
    params = pltpu.CompilerParams(vmem_limit_bytes=VMEM_BYTES)
    pay, kind_of, codes = pl.pallas_call(
        functools.partial(front, dims, size_y),
        out_shape=(pltpu.VMEM(STATE, f32), pltpu.VMEM(TILE, jnp.int32), pltpu.VMEM(TILE, jnp.int32)),
        in_specs=[hbm] * 7,
        out_specs=[vmem] * 3,
        scratch_shapes=[
            pltpu.SMEM(slot_atom.shape, jnp.int32),
            pltpu.SMEM(slot_corner.shape, jnp.int32),
            pltpu.SMEM(atom_species.shape, jnp.int32),
            pltpu.SMEM(radius.shape, f32),
            pltpu.VMEM((1, pairs), f32),
            pltpu.VMEM((size_x * size_y, size_z), f32),
            pltpu.VMEM((kinds, pairs, 1, pairs), f32),
            pltpu.SemaphoreType.DMA((7,)),
        ],
        compiler_params=params,
    )(
        *(
            pltpu.with_memory_space_constraint(x, pltpu.HBM)
            for x in (
                slot_atom,
                slot_corner,
                atom_species,
                radius,
                density_matrix,
                potential.reshape(size_x * size_y, size_z),
                coulomb.transpose(1, 0, 2),
            )
        )
    )
    bands = projections[0].transpose(1, 0, 2)
    delta, stack = pl.pallas_call(
        prepare,
        out_shape=(
            pltpu.VMEM((shapes * CODES, 2 * LANES), f32),
            pltpu.VMEM((3 * LANES, bands.shape[2]), bf16),
        ),
        in_specs=[vmem] * 3,
        out_specs=[vmem] * 2,
        compiler_params=params,
        cost_estimate=pl.CostEstimate(flops=500000, bytes_accessed=500000, transcendentals=0),
    )(kind_of, delta_table.transpose(1, 0, 2), bands)
    for axis in (0, 1):
        pay = pl.pallas_call(
            functools.partial(merge, axis, dims[axis]),
            out_shape=pltpu.VMEM(STATE, f32),
            out_specs=vmem,
            compiler_params=params,
        )(*exchange(pay, dims, axis))
    dh, applied = pl.pallas_call(
        functools.partial(back, 2, dims[2]),
        out_shape=(jax.ShapeDtypeStruct(density_matrix.shape, f32), jax.ShapeDtypeStruct(bands.shape, f32)),
        out_specs=[vmem] * 2,
        compiler_params=params,
    )(*exchange(pay, dims, 2), delta, codes, stack)
    return dh, applied.transpose(1, 0, 2)[None]


def solution(mesh):
    return jax.shard_map(
        local,
        mesh=mesh,
        in_specs=(
            P("gx", "gy", "gz"),
            P(AXES, None),
            P(),
            P(),
            P(),
            P(),
            P(AXES, None),
            P(None, AXES, None),
            P(AXES),
            P(AXES, None, None, None),
        ),
        out_specs=(P(AXES, None), P(AXES, None, None, None)),
        check_vma=False,
    )
```
